512 devices in a mesh: gx: 32 (over y, x_lo, core), gy: 16 (over z, x_hi).
Axes of the slice: x: 4 (x_hi: 2, x_lo: 2; x = x_hi * 2 + x_lo), y: 8, z: 8, core: 2. Of those that a mesh axis runs over, the one named last changes fastest.
Arguments:
- mass_per_volume: float32 [256, 128, 128], P('gx', 'gy'), may hold values from 0.4 to 2.5
- velocity: float32 [3, 256, 128, 128], P(None, 'gx', 'gy'), may hold values from -3 to 3
- thermal_stress: float32 [256, 128, 128], P('gx', 'gy'), may hold values from 0.06 to 1.5
- magnetic: float32 [3, 256, 128, 128], P(None, 'gx', 'gy'), may hold values from -4.8 to 4.8, as said below
Outputs:
- density_out: float32 [256, 128, 128], P('gx', 'gy')
- velocity_out: float32 [3, 256, 128, 128], P(None, 'gx', 'gy')
- pressure_out: float32 [256, 128, 128], P('gx', 'gy')
- magnetic_out: float32 [3, 256, 128, 128], P(None, 'gx', 'gy')
The draws below stay inside these ranges and needn't reach their ends.
Inputs may be any that keep to these rules, and one draw needn't show every extreme that they name: magnetic has zero discrete divergence in every cell: the sum over c of b_c at i+1 minus b_c at i along c vanishes up to rounding.
All inputs are finite; a program needn't handle non-finite values.
Results may differ from the reference program's by a relative error of at most 0.0003.
Values sent between devices are 32-bit elements; how exact they have to be, the bound alone decides.
No kernel may reach another device: no remote copies, remote signals or barrier semaphores. Data moves between devices by JAX's collectives and lax.ppermute only.
A program may use at most 128 MiB of HBM per device.

```python
import math
import jax
import jax.numpy as jnp
from jax import lax

CX = 8
NZ = 128
SECTIONS = 4
SUPER_SECTIONS = 8
NX = 256
NY = 128


def draw_magnetic(key, part):
    potential = jnp.clip(0.35 * jax.random.normal(key, (3, NX, NY, NZ), jnp.float32), -1.2, 1.2)
    vector_x = potential[0]
    vector_y = potential[1]
    vector_z = potential[2]
    face_x = jnp.roll(vector_z, -1, 1) - vector_z - (jnp.roll(vector_y, -1, 2) - vector_y)
    face_y = jnp.roll(vector_x, -1, 2) - vector_x - (jnp.roll(vector_z, -1, 0) - vector_z)
    face_z = jnp.roll(vector_y, -1, 0) - vector_y - (jnp.roll(vector_x, -1, 1) - vector_x)
    return jnp.stack([face_x, face_y, face_z])


def shard_levels(own_key, shape, cuts, least, largest):
    loudness, own = 1.0, jax.random.fold_in(own_key, 6)
    for axis_at, blocks in cuts:
        heights = jnp.exp(jax.random.uniform(jax.random.fold_in(own, axis_at), (blocks,), jnp.float32, least / len(cuts), largest / len(cuts)))
        loudness = loudness * jnp.repeat(heights, shape[axis_at] // blocks).reshape([-1 if axis == axis_at else 1 for axis in range(len(shape))])
    return loudness


def normal_values(stream_key, shape, scale, reach, pieces=(), kind=jnp.bfloat16):
    entries = scale * jax.random.normal(stream_key, shape, jnp.float32)
    if pieces:
        entries = entries * shard_levels(stream_key, shape, pieces, -0.22, 0.18)
    return jnp.clip(entries, -reach, reach).astype(kind)


def setup_inputs(seed: int = 0) -> dict:
    streams_of = jax.random.split(jax.random.key(seed), 5)
    mass_per_volume = jnp.clip(jnp.exp(math.log(2.5) - 1.8325814 * jax.random.uniform(streams_of[0], (NX, NY, NZ), jnp.float32) ** shard_levels(streams_of[0], (NX, NY, NZ), ((0, 32), (1, 16)), -0.2, 0.2)), 0.4, 2.5)
    velocity = normal_values(streams_of[1], (3, NX, NY, NZ), 0.5, 3.0, ((1, 32), (2, 16)), jnp.float32)
    thermal_stress = jnp.clip(jnp.exp(math.log(1.5) - 3.218876 * jax.random.uniform(streams_of[2], (NX, NY, NZ), jnp.float32) ** shard_levels(streams_of[2], (NX, NY, NZ), ((0, 32), (1, 16)), -0.2, 0.2)), 0.06, 1.5)
    magnetic = draw_magnetic(jax.random.fold_in(streams_of[4], 71), 0)
    return {"mass_per_volume": mass_per_volume, "velocity": velocity, "thermal_stress": thermal_stress, "magnetic": magnetic}


GAMMA_RATIO = 5.0 / 3.0
TIME_STEP = 0.04
SUPER_TIME = 0.08
DENSITY_FLOOR = 0.5
PRESSURE_FLOOR = 0.1
FIELD_FLOOR = 0.05

def adjacent_zone(a, dimension, k):
    return jnp.roll(a, -k, dimension)

def minmod(lower, upper):
    return 0.5 * (jnp.sign(lower) + jnp.sign(upper)) * jnp.minimum(jnp.abs(lower), jnp.abs(upper))

def wave_fluxes(mass_per_volume, velocity, thermal_stress, magnetic, adjacent_quantities):
    magnetic_sq = magnetic[0] * magnetic[0] + magnetic[1] * magnetic[1] + magnetic[2] * magnetic[2]
    kinetic = velocity[0] * velocity[0] + velocity[1] * velocity[1] + velocity[2] * velocity[2]
    whole_work_content = thermal_stress / (GAMMA_RATIO - 1.0) + 0.5 * mass_per_volume * kinetic + 0.5 * magnetic_sq
    pressure_total = thermal_stress + 0.5 * magnetic_sq
    normal_speed = velocity[adjacent_quantities]
    normal_field = magnetic[adjacent_quantities]
    projection = velocity[0] * magnetic[0] + velocity[1] * magnetic[1] + velocity[2] * magnetic[2]
    others = [zone_quantities for zone_quantities in range(3) if zone_quantities != adjacent_quantities]
    conserved = [mass_per_volume] + [mass_per_volume * velocity[zone_quantities] for zone_quantities in range(3)] + [whole_work_content] + [magnetic[zone_quantities] for zone_quantities in others]
    momentum_fluxes = []
    for zone_quantities in range(3):
        momentum_term = mass_per_volume * normal_speed * velocity[zone_quantities] - normal_field * magnetic[zone_quantities]
        if zone_quantities == adjacent_quantities:
            momentum_term = momentum_term + pressure_total
        momentum_fluxes.append(momentum_term)
    fluxes = [mass_per_volume * normal_speed] + momentum_fluxes
    fluxes = fluxes + [(whole_work_content + pressure_total) * normal_speed - normal_field * projection]
    fluxes = fluxes + [normal_speed * magnetic[zone_quantities] - velocity[zone_quantities] * normal_field for zone_quantities in others]
    signal = jnp.abs(normal_speed) + jnp.sqrt((GAMMA_RATIO * thermal_stress + magnetic_sq) / mass_per_volume)
    return (conserved, fluxes, signal)

def face_fluxes(mass_per_volume, velocity, thermal_stress, cell_field, face_field, adjacent_quantities):
    primitive = [mass_per_volume] + list(velocity) + [thermal_stress] + list(cell_field)
    lower_states = []
    upper_states = []
    for n in range(8):
        if n == 5 + adjacent_quantities:
            lower_states.append(face_field[adjacent_quantities])
            upper_states.append(face_field[adjacent_quantities])
        else:
            quantity = primitive[n]
            gradient = minmod(quantity - adjacent_zone(quantity, adjacent_quantities, -1), adjacent_zone(quantity, adjacent_quantities, 1) - quantity)
            lower_states.append(adjacent_zone(quantity + 0.5 * gradient, adjacent_quantities, -1))
            upper_states.append(quantity - 0.5 * gradient)
    conserved_lower, flux_lower, signal_lower = wave_fluxes(lower_states[0], lower_states[1:4], lower_states[4], lower_states[5:8], adjacent_quantities)
    conserved_upper, flux_upper, signal_upper = wave_fluxes(upper_states[0], upper_states[1:4], upper_states[4], upper_states[5:8], adjacent_quantities)
    signal = jnp.maximum(signal_lower, signal_upper)
    return [0.5 * (flux_lower[n] + flux_upper[n]) - 0.5 * signal * (conserved_upper[n] - conserved_lower[n]) for n in range(7)]

def hyperbolic(mass_per_volume, velocity, thermal_stress, face_field):
    cell_field = [0.5 * (face_field[zone_quantities] + adjacent_zone(face_field[zone_quantities], zone_quantities, 1)) for zone_quantities in range(3)]
    momentum = [mass_per_volume * velocity[zone_quantities] for zone_quantities in range(3)]
    kinetic = velocity[0] * velocity[0] + velocity[1] * velocity[1] + velocity[2] * velocity[2]
    magnetic_sq = cell_field[0] * cell_field[0] + cell_field[1] * cell_field[1] + cell_field[2] * cell_field[2]
    whole_work_content = thermal_stress / (GAMMA_RATIO - 1.0) + 0.5 * mass_per_volume * kinetic + 0.5 * magnetic_sq
    conserved = [mass_per_volume] + momentum + [whole_work_content]
    directional = [face_fluxes(mass_per_volume, velocity, thermal_stress, cell_field, face_field, adjacent_quantities) for adjacent_quantities in range(3)]
    updated = []
    for n in range(5):
        change = conserved[n]
        for adjacent_quantities in range(3):
            change = change - TIME_STEP * (adjacent_zone(directional[adjacent_quantities][n], adjacent_quantities, 1) - directional[adjacent_quantities][n])
        updated.append(change)

    def induction(adjacent_quantities, zone_quantities):
        others = [e for e in range(3) if e != adjacent_quantities]
        return directional[adjacent_quantities][5 + others.index(zone_quantities)]
    x_flux_y = induction(0, 1)
    y_flux_x = induction(1, 0)
    x_flux_z = induction(0, 2)
    z_flux_x = induction(2, 0)
    y_flux_z = induction(1, 2)
    z_flux_y = induction(2, 1)
    edge_z = 0.25 * (adjacent_zone(y_flux_x, 0, -1) + y_flux_x - adjacent_zone(x_flux_y, 1, -1) - x_flux_y)
    edge_y = 0.25 * (adjacent_zone(x_flux_z, 2, -1) + x_flux_z - adjacent_zone(z_flux_x, 0, -1) - z_flux_x)
    edge_x = 0.25 * (adjacent_zone(z_flux_y, 1, -1) + z_flux_y - adjacent_zone(y_flux_z, 2, -1) - y_flux_z)
    new_face = [face_field[0] - TIME_STEP * (adjacent_zone(edge_z, 1, 1) - edge_z) + TIME_STEP * (adjacent_zone(edge_y, 2, 1) - edge_y), face_field[1] - TIME_STEP * (adjacent_zone(edge_x, 2, 1) - edge_x) + TIME_STEP * (adjacent_zone(edge_z, 0, 1) - edge_z), face_field[2] - TIME_STEP * (adjacent_zone(edge_y, 0, 1) - edge_y) + TIME_STEP * (adjacent_zone(edge_x, 1, 1) - edge_x)]
    floored = jnp.maximum(updated[0], DENSITY_FLOOR)
    new_velocity = [updated[1 + zone_quantities] / floored for zone_quantities in range(3)]
    new_cell = [0.5 * (new_face[zone_quantities] + adjacent_zone(new_face[zone_quantities], zone_quantities, 1)) for zone_quantities in range(3)]
    kinetic_new = updated[1] * new_velocity[0] + updated[2] * new_velocity[1] + updated[3] * new_velocity[2]
    magnetic_new = new_cell[0] * new_cell[0] + new_cell[1] * new_cell[1] + new_cell[2] * new_cell[2]
    internal = updated[4] - 0.5 * kinetic_new - 0.5 * magnetic_new
    new_pressure = jnp.maximum((GAMMA_RATIO - 1.0) * internal, PRESSURE_FLOOR)
    return (floored, new_velocity, new_pressure, new_face)

def coefficients(mass_per_volume, thermal_stress, face_field):
    plasma_thermal_level = thermal_stress / mass_per_volume
    thermal_diffusion_coefficient = plasma_thermal_level * plasma_thermal_level * jnp.sqrt(plasma_thermal_level)
    cell_field = [0.5 * (face_field[zone_quantities] + adjacent_zone(face_field[zone_quantities], zone_quantities, 1)) for zone_quantities in range(3)]
    coupling = []
    for adjacent_quantities in range(3):
        components = []
        for zone_quantities in range(3):
            if zone_quantities == adjacent_quantities:
                components.append(face_field[adjacent_quantities])
            else:
                components.append(0.5 * (cell_field[zone_quantities] + adjacent_zone(cell_field[zone_quantities], adjacent_quantities, -1)))
        magnitude = components[0] * components[0] + components[1] * components[1] + components[2] * components[2]
        factor = 0.5 * (thermal_diffusion_coefficient + adjacent_zone(thermal_diffusion_coefficient, adjacent_quantities, -1)) / jnp.maximum(magnitude, FIELD_FLOOR)
        coupling.append([factor * face_field[adjacent_quantities] * components[zone_quantities] for zone_quantities in range(3)])
    return coupling

def conduction(whole_work_content, mass_per_volume, coupling):
    plasma_thermal_level = (GAMMA_RATIO - 1.0) * whole_work_content / mass_per_volume
    middle_derivative = [0.5 * (adjacent_zone(plasma_thermal_level, zone_quantities, 1) - adjacent_zone(plasma_thermal_level, zone_quantities, -1)) for zone_quantities in range(3)]
    result = jnp.zeros_like(whole_work_content)
    for adjacent_quantities in range(3):
        clipped_derivatives = []
        for zone_quantities in range(3):
            if zone_quantities == adjacent_quantities:
                clipped_derivatives.append(plasma_thermal_level - adjacent_zone(plasma_thermal_level, adjacent_quantities, -1))
            else:
                clipped_derivatives.append(0.5 * (middle_derivative[zone_quantities] + adjacent_zone(middle_derivative[zone_quantities], adjacent_quantities, -1)))
        heat_flux = -(coupling[adjacent_quantities][0] * clipped_derivatives[0] + coupling[adjacent_quantities][1] * clipped_derivatives[1] + coupling[adjacent_quantities][2] * clipped_derivatives[2])
        result = result - (adjacent_zone(heat_flux, adjacent_quantities, 1) - heat_flux)
    return result

def super_step(whole_work_content, initial_rate, operator):
    b = [1.0 / 3.0, 1.0 / 3.0, 1.0 / 3.0] + [(j * j + j - 2.0) / (2.0 * j * (j + 1.0)) for j in range(3, SUPER_SECTIONS + 1)]
    base_rate = 4.0 / (SUPER_SECTIONS * SUPER_SECTIONS + SUPER_SECTIONS - 2.0)
    earlier = whole_work_content
    latest = whole_work_content + b[1] * base_rate * SUPER_TIME * initial_rate
    for j in range(2, SECTIONS + 1):
        factor_prev = (2.0 * j - 1.0) / j * b[j] / b[j - 1]
        factor_back = -(j - 1.0) / j * b[j] / b[j - 2]
        factor_rate = factor_prev * base_rate
        factor_zero = -(1.0 - b[j - 1]) * factor_rate
        advanced = factor_prev * latest + factor_back * earlier + (1.0 - factor_prev - factor_back) * whole_work_content + factor_rate * SUPER_TIME * operator(latest) + factor_zero * SUPER_TIME * initial_rate
        earlier = latest
        latest = advanced
    return latest

def advance(stacked):
    mass_per_volume, velocity, thermal_stress, face_field = hyperbolic(stacked[0], [stacked[1], stacked[2], stacked[3]], stacked[4], [stacked[5], stacked[6], stacked[7]])
    coupling = coefficients(mass_per_volume, thermal_stress, face_field)
    whole_work_content = thermal_stress / (GAMMA_RATIO - 1.0)
    initial_rate = conduction(whole_work_content, mass_per_volume, coupling)
    closing = super_step(whole_work_content, initial_rate, lambda e: conduction(e, mass_per_volume, coupling))
    return jnp.stack([mass_per_volume] + velocity + [(GAMMA_RATIO - 1.0) * closing] + face_field)

def reference(mass_per_volume, velocity, thermal_stress, magnetic):
    stacked = jnp.concatenate([mass_per_volume[None], velocity, thermal_stress[None], magnetic], axis=0)
    margin = 3 + SECTIONS

    def one_slab(offset):
        row_index = (jnp.arange(CX + 2 * margin, dtype=jnp.int32) + offset - margin) % NX
        window_state = jnp.take(stacked, row_index.astype(jnp.int32), axis=1)
        return advance(window_state)[:, margin:margin + CX]
    starts = jnp.arange(NX // CX, dtype=jnp.int32) * CX
    blocks = lax.map(one_slab, starts)
    result = jnp.moveaxis(blocks, 0, 1).reshape(8, NX, NY, NZ)
    return (result[0], result[1:4], result[4], result[5:8])
```

```python
import functools

import jax
import jax.numpy as jnp
from jax import lax
from jax.experimental import pallas as pl
from jax.experimental.pallas import tpu as pltpu
from jax.sharding import PartitionSpec as P

SECTIONS = 4
SUPER_SECTIONS = 8
GAMMA_RATIO = 5.0 / 3.0
TIME_STEP = 0.04
SUPER_TIME = 0.08
DENSITY_FLOOR = 0.5
PRESSURE_FLOOR = 0.1
FIELD_FLOOR = 0.05

OWN = 8
RIM = 2 + SECTIONS
W = OWN + 2 * RIM
NZ = 128
PAD = 32
ROWS = PAD + W * W + 48
SENT = RIM * W
MID = OWN * W


def split_fields(mass_ref, velocity_ref, stress_ref, magnetic_ref, x):
    fields = [mass_ref[x]] + [velocity_ref[c, x] for c in range(3)]
    return fields + [stress_ref[x]] + [magnetic_ref[c, x] for c in range(3)]


def pack_kernel(mass_ref, velocity_ref, stress_ref, magnetic_ref, low_ref, high_ref):
    for x in range(OWN):
        fields = split_fields(mass_ref, velocity_ref, stress_ref, magnetic_ref, x)
        for n, value in enumerate(fields):
            low_ref[n, RIM * x : RIM * (x + 1)] = value[:RIM]
            high_ref[n, RIM * x : RIM * (x + 1)] = value[OWN - RIM :]


def widen_kernel(
    mass_ref, velocity_ref, stress_ref, magnetic_ref, left_ref, right_ref, mid_ref, low_ref, high_ref
):
    for x in range(OWN):
        fields = split_fields(mass_ref, velocity_ref, stress_ref, magnetic_ref, x)
        for n, value in enumerate(fields):
            left = left_ref[n, RIM * x : RIM * (x + 1)]
            right = right_ref[n, RIM * x : RIM * (x + 1)]
            targets = [(mid_ref, x * W)]
            if x < RIM:
                targets.append((low_ref, x * W))
            if x >= OWN - RIM:
                targets.append((high_ref, (x - OWN + RIM) * W))
            for ref, at in targets:
                ref[n, at : at + RIM] = left
                ref[n, at + RIM : at + RIM + OWN] = value
                ref[n, at + RIM + OWN : at + W] = right


def up(a):
    return pltpu.roll(a, NZ - 1, 1)


def down(a):
    return pltpu.roll(a, 1, 1)


def limited(value, below, above):
    slope = jnp.minimum(jnp.maximum(below, jnp.minimum(above, 0.0)), jnp.maximum(above, 0.0))
    half = 0.5 * slope
    return value - half, value + half


def state_terms(state, field, d):
    density, velocity, pressure = state[0], state[1:4], state[4]
    magnetic_sq = field[0] * field[0] + field[1] * field[1] + field[2] * field[2]
    projection = velocity[0] * field[0] + velocity[1] * field[1] + velocity[2] * field[2]
    momentum = [density * velocity[c] for c in range(3)]
    twice_kinetic = (
        momentum[0] * velocity[0] + momentum[1] * velocity[1] + momentum[2] * velocity[2]
    )
    half_sq = 0.5 * magnetic_sq
    total_pressure = pressure + half_sq
    energy = 1.5 * pressure + (0.5 * twice_kinetic + half_sq)
    speed = velocity[d]
    wave_arg = GAMMA_RATIO * pressure + magnetic_sq
    signal = jnp.abs(speed) + wave_arg * lax.rsqrt(wave_arg * density)
    others = [c for c in range(3) if c != d]
    conserved = [density] + momentum + [energy] + [field[c] for c in others]
    carried = [momentum[d]]
    for c in range(3):
        term = momentum[d] * velocity[c]
        carried.append(term + total_pressure if c == d else term)
    carried.append((energy + total_pressure) * speed)
    carried += [speed * field[c] for c in others]
    return conserved, carried, signal, projection


def twice_flux(lower, upper, normal, d):
    others = [c for c in range(3) if c != d]

    def field_of(state):
        field = [normal, normal, normal]
        for at, c in enumerate(others):
            field[c] = state[5 + at]
        return field

    field_low, field_up = field_of(lower), field_of(upper)
    u_low, f_low, s_low, j_low = state_terms(lower, field_low, d)
    u_up, f_up, s_up, j_up = state_terms(upper, field_up, d)
    signal = jnp.maximum(s_low, s_up)
    tension = [None]
    for c in range(3):
        tension.append(field_low[c] + field_up[c])
    tension.append(j_low + j_up)
    tension += [lower[1 + c] + upper[1 + c] for c in others]
    result = []
    for n in range(7):
        central = f_low[n] + f_up[n]
        if tension[n] is not None:
            central = central - normal * tension[n]
        result.append(central - signal * (u_up[n] - u_low[n]))
    return result


def tiles(first, last):
    begin = first * W // 8 * 8
    return begin, -(-(last * W - begin) // 8)


def each_tile(first, last, body):
    begin, count = tiles(first, last)

    def step(i, carry):
        body(pl.multiple_of(PAD + begin + i * 8, 8))
        return carry

    lax.fori_loop(0, count, step, 0)


def main_kernel(
    before_ref,
    mid_ref,
    after_ref,
    density_out,
    velocity_out,
    pressure_out,
    magnetic_out,
    q,
    hi,
    gx,
    gy,
    gz,
    edge,
    face,
    cell,
    coupling,
    heat,
):
    def at(ref, n, r, offset=0):
        return ref[n, pl.ds(r + offset, 8), :]

    def put(ref, n, r, value):
        ref[n, pl.ds(r, 8), :] = value

    for n in range(8):
        q[n, PAD : PAD + SENT] = before_ref[n]
        q[n, PAD + SENT : PAD + SENT + MID] = mid_ref[n]
        q[n, PAD + SENT + MID : PAD + W * W] = after_ref[n]

    def cell_fields(r):
        put(q, 8, r, 0.5 * (at(q, 5, r) + at(q, 5, r, W)))
        put(q, 9, r, 0.5 * (at(q, 6, r) + at(q, 6, r, 1)))
        bz = at(q, 7, r)
        put(q, 10, r, 0.5 * (bz + up(bz)))

    each_tile(0, W, cell_fields)

    def side_fluxes(d, offset, target):
        names = list(range(5)) + [8 + c for c in range(3) if c != d]

        def body(r):
            upper = []
            for n, name in enumerate(names):
                value = at(q, name, r)
                low, high = limited(
                    value, value - at(q, name, r, -offset), at(q, name, r, offset) - value
                )
                upper.append(low)
                put(hi, n, r, high)
            lower = [at(hi, n, r, -offset) for n in range(7)]
            for n, value in enumerate(twice_flux(lower, upper, at(q, 5 + d, r), d)):
                put(target, n, r, value)

        each_tile(1, W - 1, body)

    side_fluxes(0, W, gx)
    side_fluxes(1, 1, gy)

    def height_fluxes(r):
        lower, upper = [], []
        for name in list(range(5)) + [8, 9]:
            value = at(q, name, r)
            below = value - down(value)
            low, high = limited(value, below, up(below))
            upper.append(low)
            lower.append(down(high))
        flux = twice_flux(lower, upper, at(q, 7, r), 2)
        for n in range(5):
            put(gz, n, r, up(flux[n]) - flux[n])
        put(gz, 5, r, flux[5])
        put(gz, 6, r, flux[6])

    each_tile(1, W - 1, height_fluxes)

    quarter = 0.125 * TIME_STEP

    def edges(r):
        fx_z = at(gx, 6, r)
        fy_z = at(gy, 6, r)
        put(
            edge, 0, r, quarter * (at(gz, 6, r, -1) + at(gz, 6, r) - down(fy_z) - fy_z)
        )
        put(
            edge, 1, r, quarter * (down(fx_z) + fx_z - at(gz, 5, r, -W) - at(gz, 5, r))
        )
        put(
            edge,
            2,
            r,
            quarter * (at(gy, 5, r, -W) + at(gy, 5, r) - at(gx, 5, r, -1) - at(gx, 5, r)),
        )

    each_tile(2, W - 1, edges)

    def new_faces(r):
        ex, ey, ez = at(edge, 0, r), at(edge, 1, r), at(edge, 2, r)
        put(face, 0, r, at(q, 5, r) - (at(edge, 2, r, 1) - ez) + (up(ey) - ey))
        put(face, 1, r, at(q, 6, r) - (up(ex) - ex) + (at(edge, 2, r, W) - ez))
        put(face, 2, r, at(q, 7, r) - (at(edge, 1, r, W) - ey) + (at(edge, 0, r, 1) - ex))

    each_tile(2, W - 1, new_faces)

    def new_cells(r):
        density = at(q, 0, r)
        momentum = [density * at(q, 1 + c, r) for c in range(3)]
        twice_kinetic = (
            momentum[0] * at(q, 1, r) + momentum[1] * at(q, 2, r) + momentum[2] * at(q, 3, r)
        )
        field_sq = (
            at(q, 8, r) * at(q, 8, r) + at(q, 9, r) * at(q, 9, r) + at(q, 10, r) * at(q, 10, r)
        )
        energy = 1.5 * at(q, 4, r) + 0.5 * (twice_kinetic + field_sq)
        updated = []
        for n, value in enumerate([density] + momentum + [energy]):
            change = (at(gx, n, r, W) - at(gx, n, r)) + (at(gy, n, r, 1) - at(gy, n, r))
            updated.append(value - (0.5 * TIME_STEP) * (change + at(gz, n, r)))
        floored = jnp.maximum(updated[0], DENSITY_FLOOR)
        inverse = 1.0 / floored
        velocity = [updated[1 + c] * inverse for c in range(3)]
        bz = at(face, 2, r)
        field = [
            0.5 * (at(face, 0, r) + at(face, 0, r, W)),
            0.5 * (at(face, 1, r) + at(face, 1, r, 1)),
            0.5 * (bz + up(bz)),
        ]
        twice_kinetic = (
            updated[1] * velocity[0] + updated[2] * velocity[1] + updated[3] * velocity[2]
        )
        field_sq = field[0] * field[0] + field[1] * field[1] + field[2] * field[2]
        internal = updated[4] - 0.5 * (twice_kinetic + field_sq)
        pressure = jnp.maximum((GAMMA_RATIO - 1.0) * internal, PRESSURE_FLOOR)
        temperature = pressure * inverse
        put(cell, 0, r, floored)
        for c in range(3):
            put(cell, 1 + c, r, velocity[c])
            put(cell, 6 + c, r, field[c])
        put(cell, 4, r, inverse)
        put(cell, 5, r, temperature * temperature * jnp.sqrt(temperature))
        put(heat, 0, r, pressure)
        put(heat, 4, r, temperature)
        put(heat, 5, r, up(temperature) - down(temperature))

    each_tile(2, W - 2, new_cells)

    def couple(r):
        own_field = [at(cell, 6 + c, r) for c in range(3)]
        own_conduct = at(cell, 5, r)
        for d in range(3):
            if d < 2:
                offset = -W if d == 0 else -1
                beside = [at(cell, 6 + c, r, offset) for c in range(3)]
                conduct = at(cell, 5, r, offset)
            else:
                beside = [down(a) for a in own_field]
                conduct = down(own_conduct)
            normal = at(face, d, r)
            parts = [normal if c == d else 0.5 * (own_field[c] + beside[c]) for c in range(3)]
            size = parts[0] * parts[0] + parts[1] * parts[1] + parts[2] * parts[2]
            factor = 0.5 * (own_conduct + conduct) / jnp.maximum(size, FIELD_FLOOR) * normal
            mixed = 0.25 * factor
            for c in range(3):
                put(coupling, 3 * d + c, r, (factor if c == d else mixed) * parts[c])

    each_tile(3, W - 2, couple)

    def heat_fluxes(r):
        t = at(heat, 4, r)
        t_above_x = at(heat, 4, r, W)
        t_below_x = at(heat, 4, r, -W)
        t_above_y = at(heat, 4, r, 1)
        t_below_y = at(heat, 4, r, -1)
        along_x = t_above_x - t_below_x
        along_y = t_above_y - t_below_y
        along_z = at(heat, 5, r)
        beside_x = at(heat, 4, r, W - 1) - at(heat, 4, r, -W - 1)
        beside_y = at(heat, 4, r, 1 - W) - at(heat, 4, r, -1 - W)
        k = [at(coupling, n, r) for n in range(9)]
        qx = (
            k[0] * (t - t_below_x)
            + k[1] * (along_y + beside_y)
            + k[2] * (along_z + at(heat, 5, r, -W))
        )
        qy = (
            k[3] * (along_x + beside_x)
            + k[4] * (t - t_below_y)
            + k[5] * (along_z + at(heat, 5, r, -1))
        )
        qz = (
            k[6] * (along_x + down(along_x))
            + k[7] * (along_y + down(along_y))
            + k[8] * (t - down(t))
        )
        put(heat, 6, r, qx)
        put(heat, 7, r, qy)
        put(heat, 8, r, up(qz) - qz)

    def rate_at(r):
        return (
            (at(heat, 6, r, W) - at(heat, 6, r))
            + (at(heat, 7, r, 1) - at(heat, 7, r))
            + at(heat, 8, r)
        )

    b = [1.0 / 3.0] * 3 + [(j * j + j - 2.0) / (2.0 * j * (j + 1.0)) for j in range(3, SECTIONS + 1)]
    base_rate = 4.0 / (SUPER_SECTIONS * SUPER_SECTIONS + SUPER_SECTIONS - 2.0)
    scale = (GAMMA_RATIO - 1.0) * SUPER_TIME * base_rate

    def section(j, r):
        rate = rate_at(r)
        if j == 1:
            put(heat, 9, r, rate)
            return at(heat, 0, r) + (b[1] * scale) * rate
        mu = (2.0 * j - 1.0) / j * b[j] / b[j - 1]
        nu = -(j - 1.0) / j * b[j] / b[j - 2]
        if j == 2:
            base = (1.0 - mu) * at(heat, 0, r)
        else:
            base = nu * at(heat, j - 2, r) + (1.0 - mu - nu) * at(heat, 0, r)
        return (
            mu * at(heat, j - 1, r)
            + base
            + (mu * scale) * rate
            - ((1.0 - b[j - 1]) * mu * scale) * at(heat, 9, r)
        )

    for j in range(1, SECTIONS):
        each_tile(2 + j, W - 1 - j, heat_fluxes)

        def advance(r, j=j):
            pressure = section(j, r)
            put(heat, j, r, pressure)
            temperature = pressure * at(cell, 4, r)
            put(heat, 4, r, temperature)
            put(heat, 5, r, up(temperature) - down(temperature))

        each_tile(2 + j, W - 2 - j, advance)

    each_tile(2 + SECTIONS, W - 1 - SECTIONS, heat_fluxes)

    def finish(x, carry):
        r = PAD + (x + RIM) * W + RIM
        pressure_out[x] = section(SECTIONS, r)
        density_out[x] = at(cell, 0, r)
        for c in range(3):
            velocity_out[c, x] = at(cell, 1 + c, r)
            magnetic_out[c, x] = at(face, c, r)
        return carry

    lax.fori_loop(0, OWN, finish, 0)


def shift(a, axis, by):
    count = lax.axis_size(axis)
    return lax.ppermute(a, axis, [(i, (i + by) % count) for i in range(count)])


def local(mass_per_volume, velocity, thermal_stress, magnetic):
    f32 = jnp.float32
    shaped = functools.partial(jax.ShapeDtypeStruct, dtype=f32)
    own = (mass_per_volume, velocity, thermal_stress, magnetic)
    to_low, to_high = pl.pallas_call(
        pack_kernel, out_shape=(shaped((8, OWN * RIM, NZ)), shaped((8, OWN * RIM, NZ))), name="pack"
    )(*own)
    left = shift(to_high, "gy", 1)
    right = shift(to_low, "gy", -1)
    mid, to_low, to_high = pl.pallas_call(
        widen_kernel,
        out_shape=(shaped((8, MID, NZ)), shaped((8, SENT, NZ)), shaped((8, SENT, NZ))),
        name="widen",
    )(*own, left, right)
    before = shift(to_high, "gx", 1)
    after = shift(to_low, "gx", -1)

    def scratch(n):
        return pltpu.VMEM((n, ROWS, NZ), f32)

    block = (OWN, OWN, NZ)
    return pl.pallas_call(
        main_kernel,
        out_shape=(shaped(block), shaped((3, *block)), shaped(block), shaped((3, *block))),
        scratch_shapes=[scratch(n) for n in (11, 7, 7, 7, 7, 3, 3, 9, 9, 10)],
        compiler_params=pltpu.CompilerParams(vmem_limit_bytes=40 * 1024 * 1024),
        name="main",
    )(before, mid, after)


def solution(mesh):
    grid = P("gx", "gy", None)
    stacked = P(None, "gx", "gy", None)
    return jax.shard_map(
        local,
        mesh=mesh,
        in_specs=(grid, stacked, grid, stacked),
        out_specs=(grid, stacked, grid, stacked),
        check_vma=False,
    )
```

```python
import functools

import jax
import jax.numpy as jnp
from jax import lax
from jax.experimental import pallas as pl
from jax.experimental.pallas import tpu as pltpu
from jax.sharding import PartitionSpec as P

SECTIONS = 4
SUPER_SECTIONS = 8
GAMMA_RATIO = 5.0 / 3.0
TIME_STEP = 0.04
SUPER_TIME = 0.08
DENSITY_FLOOR = 0.5
PRESSURE_FLOOR = 0.1
FIELD_FLOOR = 0.05

OWN = 8
RIM = 2 + SECTIONS
W = OWN + 2 * RIM
NZ = 128
PAD = 32
ROWS = PAD + W * W + 96
SENT = RIM * W
MID = OWN * W
STATES, CELLS, COUPLE, FLOWS, ADVANCE = 184, 160, 152, 48, 184


def split_fields(mass_ref, velocity_ref, stress_ref, magnetic_ref, x):
    fields = [mass_ref[x]] + [velocity_ref[c, x] for c in range(3)]
    return fields + [stress_ref[x]] + [magnetic_ref[c, x] for c in range(3)]


def pack_kernel(mass_ref, velocity_ref, stress_ref, magnetic_ref, low_ref, high_ref):
    for x in range(OWN):
        fields = split_fields(mass_ref, velocity_ref, stress_ref, magnetic_ref, x)
        for n, value in enumerate(fields):
            low_ref[n, RIM * x : RIM * (x + 1)] = value[:RIM]
            high_ref[n, RIM * x : RIM * (x + 1)] = value[OWN - RIM :]


def widen_kernel(
    mass_ref, velocity_ref, stress_ref, magnetic_ref, left_ref, right_ref, mid_ref, low_ref, high_ref
):
    for x in range(OWN):
        fields = split_fields(mass_ref, velocity_ref, stress_ref, magnetic_ref, x)
        for n, value in enumerate(fields):
            left = left_ref[n, RIM * x : RIM * (x + 1)]
            right = right_ref[n, RIM * x : RIM * (x + 1)]
            targets = [(mid_ref, x * W)]
            if x < RIM:
                targets.append((low_ref, x * W))
            if x >= OWN - RIM:
                targets.append((high_ref, (x - OWN + RIM) * W))
            for ref, at in targets:
                ref[n, at : at + RIM] = left
                ref[n, at + RIM : at + RIM + OWN] = value
                ref[n, at + RIM + OWN : at + W] = right


def up(a):
    return pltpu.roll(a, NZ - 1, 1)


def down(a, by=1):
    return pltpu.roll(a, by, 1)


def half_slope(below, above):
    slope = jnp.minimum(jnp.maximum(below, jnp.minimum(above, 0.0)), jnp.maximum(above, 0.0))
    return 0.5 * slope


def state_terms(state, field, d):
    density, velocity, pressure = state[0], state[1:4], state[4]
    magnetic_sq = field[0] * field[0] + field[1] * field[1] + field[2] * field[2]
    projection = velocity[0] * field[0] + velocity[1] * field[1] + velocity[2] * field[2]
    momentum = [density * velocity[c] for c in range(3)]
    twice_kinetic = (
        momentum[0] * velocity[0] + momentum[1] * velocity[1] + momentum[2] * velocity[2]
    )
    half_sq = 0.5 * magnetic_sq
    total_pressure = pressure + half_sq
    energy = 1.5 * pressure + (0.5 * twice_kinetic + half_sq)
    speed = velocity[d]
    wave_arg = GAMMA_RATIO * pressure + magnetic_sq
    signal = jnp.abs(speed) + wave_arg * lax.rsqrt(wave_arg * density)
    others = [c for c in range(3) if c != d]
    conserved = [density] + momentum + [energy] + [field[c] for c in others]
    carried = [momentum[d]]
    for c in range(3):
        term = momentum[d] * velocity[c]
        carried.append(term + total_pressure if c == d else term)
    carried.append((energy + total_pressure) * speed)
    carried += [speed * field[c] for c in others]
    return conserved, carried, signal, projection


def twice_flux(lower, upper, normal, d):
    others = [c for c in range(3) if c != d]

    def field_of(state):
        field = [normal, normal, normal]
        for at, c in enumerate(others):
            field[c] = state[5 + at]
        return field

    field_low, field_up = field_of(lower), field_of(upper)
    u_low, f_low, s_low, j_low = state_terms(lower, field_low, d)
    u_up, f_up, s_up, j_up = state_terms(upper, field_up, d)
    signal = jnp.maximum(s_low, s_up)
    tension = [None]
    for c in range(3):
        tension.append(field_low[c] + field_up[c])
    tension.append(j_low + j_up)
    tension += [lower[1 + c] + upper[1 + c] for c in others]
    result = []
    for n in range(7):
        central = f_low[n] + f_up[n]
        if tension[n] is not None:
            central = central - normal * tension[n]
        result.append(central - signal * (u_up[n] - u_low[n]))
    return result


def each_block(first, last, rows, body):
    begin = first * W // 8 * 8
    count = -(-(last * W - begin) // rows)

    def step(i, carry):
        body((pl.multiple_of(PAD + begin + i * rows, 8), rows))
        return carry

    lax.fori_loop(0, count, step, 0)


def main_kernel(
    before_ref,
    mid_ref,
    after_ref,
    density_out,
    velocity_out,
    pressure_out,
    magnetic_out,
    q,
    hi,
    gx,
    gy,
    gz,
    edge,
    face,
    cell,
    coupling,
    heat,
):
    def at(ref, n, r, offset=0):
        return ref[n, pl.ds(r[0] + offset, r[1]), :]

    def put(ref, n, r, value):
        ref[n, pl.ds(r[0], r[1]), :] = value

    for n in range(8):
        q[n, PAD : PAD + SENT] = before_ref[n]
        q[n, PAD + SENT : PAD + SENT + MID] = mid_ref[n]
        q[n, PAD + SENT + MID : PAD + W * W] = after_ref[n]

    def cell_fields(r):
        put(q, 8, r, 0.5 * (at(q, 5, r) + at(q, 5, r, W)))
        put(q, 9, r, 0.5 * (at(q, 6, r) + at(q, 6, r, 1)))
        bz = at(q, 7, r)
        put(q, 10, r, 0.5 * (bz + up(bz)))

    each_block(0, W, 400, cell_fields)

    def side_fluxes(d, offset, target):
        names = list(range(5)) + [8 + c for c in range(3) if c != d]

        def body(r):
            upper = []
            for n, name in enumerate(names):
                value = at(q, name, r)
                half = half_slope(value - at(q, name, r, -offset), at(q, name, r, offset) - value)
                upper.append(value - half)
                put(hi, n, r, value + half)
            lower = [at(hi, n, r, -offset) for n in range(7)]
            for n, value in enumerate(twice_flux(lower, upper, at(q, 5 + d, r), d)):
                put(target, n, r, value)

        each_block(1, W - 1, 16, body)

    side_fluxes(0, W, gx)
    side_fluxes(1, 1, gy)

    def height_states(r):
        for n, name in enumerate(list(range(5)) + [8, 9]):
            value = at(q, name, r)
            before, earlier, after = down(value), down(value, 2), up(value)
            below = value - before
            put(hi, n, r, value - half_slope(below, after - value))
            put(hi, 7 + n, r, before + half_slope(before - earlier, below))

    each_block(1, W - 1, STATES, height_states)

    def height_fluxes(r):
        upper = [at(hi, n, r) for n in range(7)]
        lower = [at(hi, 7 + n, r) for n in range(7)]
        for n, value in enumerate(twice_flux(lower, upper, at(q, 7, r), 2)):
            put(gz, n, r, value)

    each_block(1, W - 1, 16, height_fluxes)

    quarter = 0.125 * TIME_STEP

    def edges(r):
        fx_z = at(gx, 6, r)
        fy_z = at(gy, 6, r)
        put(
            edge, 0, r, quarter * (at(gz, 6, r, -1) + at(gz, 6, r) - down(fy_z) - fy_z)
        )
        put(
            edge, 1, r, quarter * (down(fx_z) + fx_z - at(gz, 5, r, -W) - at(gz, 5, r))
        )
        put(
            edge,
            2,
            r,
            quarter * (at(gy, 5, r, -W) + at(gy, 5, r) - at(gx, 5, r, -1) - at(gx, 5, r)),
        )

    each_block(2, W - 1, 344, edges)

    def new_faces(r):
        ex, ey, ez = at(edge, 0, r), at(edge, 1, r), at(edge, 2, r)
        put(face, 0, r, at(q, 5, r) - (at(edge, 2, r, 1) - ez) + (up(ey) - ey))
        put(face, 1, r, at(q, 6, r) - (up(ex) - ex) + (at(edge, 2, r, W) - ez))
        put(face, 2, r, at(q, 7, r) - (at(edge, 1, r, W) - ey) + (at(edge, 0, r, 1) - ex))

    each_block(2, W - 1, 344, new_faces)

    def put_temperature(r, temperature):
        above, below = up(temperature), down(temperature)
        put(heat, 4, r, temperature)
        put(heat, 5, r, temperature + below)
        put(heat, 6, r, temperature - below)
        put(heat, 7, r, above - below)

    def new_cells(r):
        density = at(q, 0, r)
        momentum = [density * at(q, 1 + c, r) for c in range(3)]
        twice_kinetic = (
            momentum[0] * at(q, 1, r) + momentum[1] * at(q, 2, r) + momentum[2] * at(q, 3, r)
        )
        field_sq = (
            at(q, 8, r) * at(q, 8, r) + at(q, 9, r) * at(q, 9, r) + at(q, 10, r) * at(q, 10, r)
        )
        energy = 1.5 * at(q, 4, r) + 0.5 * (twice_kinetic + field_sq)
        updated = []
        for n, value in enumerate([density] + momentum + [energy]):
            change = (at(gx, n, r, W) - at(gx, n, r)) + (at(gy, n, r, 1) - at(gy, n, r))
            above = at(gz, n, r)
            updated.append(value - (0.5 * TIME_STEP) * (change + (up(above) - above)))
        floored = jnp.maximum(updated[0], DENSITY_FLOOR)
        inverse = 1.0 / floored
        velocity = [updated[1 + c] * inverse for c in range(3)]
        bz = at(face, 2, r)
        field = [
            0.5 * (at(face, 0, r) + at(face, 0, r, W)),
            0.5 * (at(face, 1, r) + at(face, 1, r, 1)),
            0.5 * (bz + up(bz)),
        ]
        twice_kinetic = (
            updated[1] * velocity[0] + updated[2] * velocity[1] + updated[3] * velocity[2]
        )
        field_sq = field[0] * field[0] + field[1] * field[1] + field[2] * field[2]
        internal = updated[4] - 0.5 * (twice_kinetic + field_sq)
        pressure = jnp.maximum((GAMMA_RATIO - 1.0) * internal, PRESSURE_FLOOR)
        temperature = pressure * inverse
        put(cell, 0, r, floored)
        for c in range(3):
            put(cell, 1 + c, r, velocity[c])
            put(cell, 6 + c, r, field[c])
        put(cell, 4, r, inverse)
        put(cell, 5, r, temperature * temperature * jnp.sqrt(temperature))
        put(heat, 0, r, pressure)
        put_temperature(r, temperature)

    each_block(2, W - 2, CELLS, new_cells)

    def couple(r):
        own_field = [at(cell, 6 + c, r) for c in range(3)]
        own_conduct = at(cell, 5, r)
        for d in range(3):
            if d < 2:
                offset = -W if d == 0 else -1
                beside = [at(cell, 6 + c, r, offset) for c in range(3)]
                conduct = at(cell, 5, r, offset)
            else:
                beside = [down(a) for a in own_field]
                conduct = down(own_conduct)
            normal = at(face, d, r)
            parts = [normal if c == d else 0.5 * (own_field[c] + beside[c]) for c in range(3)]
            size = parts[0] * parts[0] + parts[1] * parts[1] + parts[2] * parts[2]
            factor = 0.5 * (own_conduct + conduct) / jnp.maximum(size, FIELD_FLOOR) * normal
            mixed = 0.25 * factor
            for c in range(3):
                put(coupling, 3 * d + c, r, (factor if c == d else mixed) * parts[c])

    each_block(3, W - 2, COUPLE, couple)

    def heat_fluxes(r):
        t = at(heat, 4, r)
        t_below_x = at(heat, 4, r, -W)
        t_below_y = at(heat, 4, r, -1)
        along_x = at(heat, 4, r, W) - t_below_x
        along_y = at(heat, 4, r, 1) - t_below_y
        along_z = at(heat, 7, r)
        beside_x = at(heat, 4, r, W - 1) - at(heat, 4, r, -W - 1)
        beside_y = at(heat, 4, r, 1 - W) - at(heat, 4, r, -1 - W)
        k = [at(coupling, n, r) for n in range(9)]
        qx = (
            k[0] * (t - t_below_x)
            + k[1] * (along_y + beside_y)
            + k[2] * (along_z + at(heat, 7, r, -W))
        )
        qy = (
            k[3] * (along_x + beside_x)
            + k[4] * (t - t_below_y)
            + k[5] * (along_z + at(heat, 7, r, -1))
        )
        qz = (
            k[6] * (at(heat, 5, r, W) - at(heat, 5, r, -W))
            + k[7] * (at(heat, 5, r, 1) - at(heat, 5, r, -1))
            + k[8] * at(heat, 6, r)
        )
        put(heat, 8, r, qx)
        put(heat, 9, r, qy)
        put(heat, 10, r, qz)

    def rate_at(r):
        qz = at(heat, 10, r)
        return (
            (at(heat, 8, r, W) - at(heat, 8, r)) + (at(heat, 9, r, 1) - at(heat, 9, r)) + (up(qz) - qz)
        )

    b = [1.0 / 3.0] * 3 + [(j * j + j - 2.0) / (2.0 * j * (j + 1.0)) for j in range(3, SECTIONS + 1)]
    base_rate = 4.0 / (SUPER_SECTIONS * SUPER_SECTIONS + SUPER_SECTIONS - 2.0)
    scale = (GAMMA_RATIO - 1.0) * SUPER_TIME * base_rate

    def section(j, r):
        rate = rate_at(r)
        if j == 1:
            put(heat, 11, r, rate)
            return at(heat, 0, r) + (b[1] * scale) * rate
        mu = (2.0 * j - 1.0) / j * b[j] / b[j - 1]
        nu = -(j - 1.0) / j * b[j] / b[j - 2]
        if j == 2:
            base = (1.0 - mu) * at(heat, 0, r)
        else:
            base = nu * at(heat, j - 2, r) + (1.0 - mu - nu) * at(heat, 0, r)
        return (
            mu * at(heat, j - 1, r)
            + base
            + (mu * scale) * rate
            - ((1.0 - b[j - 1]) * mu * scale) * at(heat, 11, r)
        )

    for j in range(1, SECTIONS):
        each_block(2 + j, W - 1 - j, FLOWS, heat_fluxes)

        def advance(r, j=j):
            pressure = section(j, r)
            put(heat, j, r, pressure)
            put_temperature(r, pressure * at(cell, 4, r))

        each_block(2 + j, W - 2 - j, ADVANCE, advance)

    each_block(2 + SECTIONS, W - 1 - SECTIONS, FLOWS, heat_fluxes)

    for x in range(OWN):
        r = (PAD + (x + RIM) * W + RIM, OWN)
        pressure_out[x] = section(SECTIONS, r)
        density_out[x] = at(cell, 0, r)
        for c in range(3):
            velocity_out[c, x] = at(cell, 1 + c, r)
            magnetic_out[c, x] = at(face, c, r)


def main_call(before, mid, after, kernel=main_kernel, name="main"):
    def shaped(*shape):
        return jax.ShapeDtypeStruct(shape, jnp.float32)

    block = (OWN, OWN, NZ)
    return pl.pallas_call(
        kernel,
        out_shape=(shaped(*block), shaped(3, *block), shaped(*block), shaped(3, *block)),
        scratch_shapes=[
            pltpu.VMEM((n, ROWS, NZ), jnp.float32) for n in (11, 14, 7, 7, 7, 3, 3, 9, 9, 12)
        ],
        compiler_params=pltpu.CompilerParams(vmem_limit_bytes=40 * 1024 * 1024),
        name=name,
    )(before, mid, after)


def shift(a, axis, by):
    count = lax.axis_size(axis)
    return lax.ppermute(a, axis, [(i, (i + by) % count) for i in range(count)])


def local(mass_per_volume, velocity, thermal_stress, magnetic):
    f32 = jnp.float32
    shaped = functools.partial(jax.ShapeDtypeStruct, dtype=f32)
    own = (mass_per_volume, velocity, thermal_stress, magnetic)
    to_low, to_high = pl.pallas_call(
        pack_kernel, out_shape=(shaped((8, OWN * RIM, NZ)), shaped((8, OWN * RIM, NZ))), name="pack"
    )(*own)
    left = shift(to_high, "gy", 1)
    right = shift(to_low, "gy", -1)
    mid, to_low, to_high = pl.pallas_call(
        widen_kernel,
        out_shape=(shaped((8, MID, NZ)), shaped((8, SENT, NZ)), shaped((8, SENT, NZ))),
        name="widen",
    )(*own, left, right)
    before = shift(to_high, "gx", 1)
    after = shift(to_low, "gx", -1)

    return main_call(before, mid, after)


def solution(mesh):
    grid = P("gx", "gy", None)
    stacked = P(None, "gx", "gy", None)
    return jax.shard_map(
        local,
        mesh=mesh,
        in_specs=(grid, stacked, grid, stacked),
        out_specs=(grid, stacked, grid, stacked),
        check_vma=False,
    )
```

```python
import jax
import jax.numpy as jnp
from jax import lax
from jax.experimental import pallas as pl
from jax.experimental.pallas import tpu as pltpu
from jax.sharding import PartitionSpec as P

SECTIONS = 4
SUPER_SECTIONS = 8
GAMMA_RATIO = 5.0 / 3.0
TIME_STEP = 0.04
SUPER_TIME = 0.08
DENSITY_FLOOR = 0.5
PRESSURE_FLOOR = 0.1
FIELD_FLOOR = 0.05

OWN = 8
RIM = 2 + SECTIONS
W = OWN + 2 * RIM
NZ = 128
PAD = 32
ROWS = PAD + W * W + 96
SENT = RIM * W
MID = OWN * W
STATES, CELLS, COUPLE, FLOWS, ADVANCE = 184, 160, 152, 48, 184


def pack_kernel(mass_ref, velocity_ref, stress_ref, magnetic_ref, own_ref, low_ref, high_ref):
    for x in range(OWN):
        fields = [mass_ref[x]] + [velocity_ref[c, x] for c in range(3)]
        fields += [stress_ref[x]] + [magnetic_ref[c, x] for c in range(3)]
        for n, value in enumerate(fields):
            own_ref[n, OWN * x : OWN * (x + 1)] = value
            low_ref[n, RIM * x : RIM * (x + 1)] = value[:RIM]
            high_ref[n, RIM * x : RIM * (x + 1)] = value[OWN - RIM :]


def widen_kernel(own_ref, left_ref, right_ref, mid_ref, low_ref, high_ref):
    for x in range(OWN):
        targets = [(mid_ref, x * W)]
        if x < RIM:
            targets.append((low_ref, x * W))
        if x >= OWN - RIM:
            targets.append((high_ref, (x - OWN + RIM) * W))
        for n in range(8):
            left = left_ref[n, RIM * x : RIM * (x + 1)]
            value = own_ref[n, OWN * x : OWN * (x + 1)]
            right = right_ref[n, RIM * x : RIM * (x + 1)]
            for ref, at in targets:
                ref[n, at : at + RIM] = left
                ref[n, at + RIM : at + RIM + OWN] = value
                ref[n, at + RIM + OWN : at + W] = right


def up(a):
    return pltpu.roll(a, NZ - 1, 1)


def down(a, by=1):
    return pltpu.roll(a, by, 1)


def half_slope(below, above):
    slope = jnp.minimum(jnp.maximum(below, jnp.minimum(above, 0.0)), jnp.maximum(above, 0.0))
    return 0.5 * slope


def state_terms(state, field, d):
    density, velocity, pressure = state[0], state[1:4], state[4]
    magnetic_sq = field[0] * field[0] + field[1] * field[1] + field[2] * field[2]
    projection = velocity[0] * field[0] + velocity[1] * field[1] + velocity[2] * field[2]
    momentum = [density * velocity[c] for c in range(3)]
    twice_kinetic = (
        momentum[0] * velocity[0] + momentum[1] * velocity[1] + momentum[2] * velocity[2]
    )
    half_sq = 0.5 * magnetic_sq
    total_pressure = pressure + half_sq
    energy = 1.5 * pressure + (0.5 * twice_kinetic + half_sq)
    speed = velocity[d]
    wave_arg = GAMMA_RATIO * pressure + magnetic_sq
    signal = jnp.abs(speed) + wave_arg * lax.rsqrt(wave_arg * density)
    others = [c for c in range(3) if c != d]
    conserved = [density] + momentum + [energy] + [field[c] for c in others]
    carried = [momentum[d]]
    for c in range(3):
        term = momentum[d] * velocity[c]
        carried.append(term + total_pressure if c == d else term)
    carried.append((energy + total_pressure) * speed)
    carried += [speed * field[c] for c in others]
    return conserved, carried, signal, projection


def twice_flux(lower, upper, normal, d):
    others = [c for c in range(3) if c != d]

    def field_of(state):
        field = [normal, normal, normal]
        for at, c in enumerate(others):
            field[c] = state[5 + at]
        return field

    field_low, field_up = field_of(lower), field_of(upper)
    u_low, f_low, s_low, j_low = state_terms(lower, field_low, d)
    u_up, f_up, s_up, j_up = state_terms(upper, field_up, d)
    signal = jnp.maximum(s_low, s_up)
    tension = [None]
    for c in range(3):
        tension.append(field_low[c] + field_up[c])
    tension.append(j_low + j_up)
    tension += [lower[1 + c] + upper[1 + c] for c in others]
    result = []
    for n in range(7):
        central = f_low[n] + f_up[n]
        if tension[n] is not None:
            central = central - normal * tension[n]
        result.append(central - signal * (u_up[n] - u_low[n]))
    return result


def each_block(first, last, rows, body):
    begin = first * W // 8 * 8
    count = -(-(last * W - begin) // rows)

    def step(i, carry):
        body((pl.multiple_of(PAD + begin + i * rows, 8), rows))
        return carry

    lax.fori_loop(0, count, step, 0)


def main_kernel(
    before_ref,
    mid_ref,
    after_ref,
    density_out,
    velocity_out,
    pressure_out,
    magnetic_out,
    q,
    hi,
    gx,
    gy,
    gz,
    edge,
    face,
    cell,
    coupling,
    heat,
):
    def at(ref, n, r, offset=0):
        return ref[n, pl.ds(r[0] + offset, r[1]), :]

    def put(ref, n, r, value):
        ref[n, pl.ds(r[0], r[1]), :] = value

    for n in range(8):
        q[n, PAD : PAD + SENT] = before_ref[n]
        q[n, PAD + SENT : PAD + SENT + MID] = mid_ref[n]
        q[n, PAD + SENT + MID : PAD + W * W] = after_ref[n]

    def cell_fields(r):
        put(q, 8, r, 0.5 * (at(q, 5, r) + at(q, 5, r, W)))
        put(q, 9, r, 0.5 * (at(q, 6, r) + at(q, 6, r, 1)))
        bz = at(q, 7, r)
        put(q, 10, r, 0.5 * (bz + up(bz)))

    each_block(0, W, 400, cell_fields)

    def side_fluxes(d, offset, target):
        names = list(range(5)) + [8 + c for c in range(3) if c != d]

        def body(r):
            upper = []
            for n, name in enumerate(names):
                value = at(q, name, r)
                half = half_slope(value - at(q, name, r, -offset), at(q, name, r, offset) - value)
                upper.append(value - half)
                put(hi, n, r, value + half)
            lower = [at(hi, n, r, -offset) for n in range(7)]
            for n, value in enumerate(twice_flux(lower, upper, at(q, 5 + d, r), d)):
                put(target, n, r, value)

        each_block(1, W - 1, 16, body)

    side_fluxes(0, W, gx)
    side_fluxes(1, 1, gy)

    def height_states(r):
        for n, name in enumerate(list(range(5)) + [8, 9]):
            value = at(q, name, r)
            before, earlier, after = down(value), down(value, 2), up(value)
            below = value - before
            put(hi, n, r, value - half_slope(below, after - value))
            put(hi, 7 + n, r, before + half_slope(before - earlier, below))

    each_block(1, W - 1, STATES, height_states)

    def height_fluxes(r):
        upper = [at(hi, n, r) for n in range(7)]
        lower = [at(hi, 7 + n, r) for n in range(7)]
        for n, value in enumerate(twice_flux(lower, upper, at(q, 7, r), 2)):
            put(gz, n, r, value)

    each_block(1, W - 1, 16, height_fluxes)

    quarter = 0.125 * TIME_STEP

    def edges(r):
        fx_z = at(gx, 6, r)
        fy_z = at(gy, 6, r)
        put(
            edge, 0, r, quarter * (at(gz, 6, r, -1) + at(gz, 6, r) - down(fy_z) - fy_z)
        )
        put(
            edge, 1, r, quarter * (down(fx_z) + fx_z - at(gz, 5, r, -W) - at(gz, 5, r))
        )
        put(
            edge,
            2,
            r,
            quarter * (at(gy, 5, r, -W) + at(gy, 5, r) - at(gx, 5, r, -1) - at(gx, 5, r)),
        )

    each_block(2, W - 1, 344, edges)

    def new_faces(r):
        ex, ey, ez = at(edge, 0, r), at(edge, 1, r), at(edge, 2, r)
        put(face, 0, r, at(q, 5, r) - (at(edge, 2, r, 1) - ez) + (up(ey) - ey))
        put(face, 1, r, at(q, 6, r) - (up(ex) - ex) + (at(edge, 2, r, W) - ez))
        put(face, 2, r, at(q, 7, r) - (at(edge, 1, r, W) - ey) + (at(edge, 0, r, 1) - ex))

    each_block(2, W - 1, 344, new_faces)

    def put_temperature(r, temperature):
        above, below = up(temperature), down(temperature)
        put(heat, 4, r, temperature)
        put(heat, 5, r, temperature + below)
        put(heat, 6, r, temperature - below)
        put(heat, 7, r, above - below)

    def new_cells(r):
        density = at(q, 0, r)
        momentum = [density * at(q, 1 + c, r) for c in range(3)]
        twice_kinetic = (
            momentum[0] * at(q, 1, r) + momentum[1] * at(q, 2, r) + momentum[2] * at(q, 3, r)
        )
        field_sq = (
            at(q, 8, r) * at(q, 8, r) + at(q, 9, r) * at(q, 9, r) + at(q, 10, r) * at(q, 10, r)
        )
        energy = 1.5 * at(q, 4, r) + 0.5 * (twice_kinetic + field_sq)
        updated = []
        for n, value in enumerate([density] + momentum + [energy]):
            change = (at(gx, n, r, W) - at(gx, n, r)) + (at(gy, n, r, 1) - at(gy, n, r))
            above = at(gz, n, r)
            updated.append(value - (0.5 * TIME_STEP) * (change + (up(above) - above)))
        floored = jnp.maximum(updated[0], DENSITY_FLOOR)
        inverse = 1.0 / floored
        velocity = [updated[1 + c] * inverse for c in range(3)]
        bz = at(face, 2, r)
        field = [
            0.5 * (at(face, 0, r) + at(face, 0, r, W)),
            0.5 * (at(face, 1, r) + at(face, 1, r, 1)),
            0.5 * (bz + up(bz)),
        ]
        twice_kinetic = (
            updated[1] * velocity[0] + updated[2] * velocity[1] + updated[3] * velocity[2]
        )
        field_sq = field[0] * field[0] + field[1] * field[1] + field[2] * field[2]
        internal = updated[4] - 0.5 * (twice_kinetic + field_sq)
        pressure = jnp.maximum((GAMMA_RATIO - 1.0) * internal, PRESSURE_FLOOR)
        temperature = pressure * inverse
        put(cell, 0, r, floored)
        for c in range(3):
            put(cell, 1 + c, r, velocity[c])
            put(cell, 6 + c, r, field[c])
        put(cell, 4, r, inverse)
        put(cell, 5, r, temperature * temperature * jnp.sqrt(temperature))
        put(heat, 0, r, pressure)
        put_temperature(r, temperature)

    each_block(2, W - 2, CELLS, new_cells)

    def couple(r):
        own_field = [at(cell, 6 + c, r) for c in range(3)]
        own_conduct = at(cell, 5, r)
        for d in range(3):
            if d < 2:
                offset = -W if d == 0 else -1
                beside = [at(cell, 6 + c, r, offset) for c in range(3)]
                conduct = at(cell, 5, r, offset)
            else:
                beside = [down(a) for a in own_field]
                conduct = down(own_conduct)
            normal = at(face, d, r)
            parts = [normal if c == d else 0.5 * (own_field[c] + beside[c]) for c in range(3)]
            size = parts[0] * parts[0] + parts[1] * parts[1] + parts[2] * parts[2]
            factor = 0.5 * (own_conduct + conduct) / jnp.maximum(size, FIELD_FLOOR) * normal
            mixed = 0.25 * factor
            for c in range(3):
                put(coupling, 3 * d + c, r, (factor if c == d else mixed) * parts[c])

    each_block(3, W - 2, COUPLE, couple)

    def heat_fluxes(r):
        t = at(heat, 4, r)
        t_below_x = at(heat, 4, r, -W)
        t_below_y = at(heat, 4, r, -1)
        along_x = at(heat, 4, r, W) - t_below_x
        along_y = at(heat, 4, r, 1) - t_below_y
        along_z = at(heat, 7, r)
        beside_x = at(heat, 4, r, W - 1) - at(heat, 4, r, -W - 1)
        beside_y = at(heat, 4, r, 1 - W) - at(heat, 4, r, -1 - W)
        k = [at(coupling, n, r) for n in range(9)]
        qx = (
            k[0] * (t - t_below_x)
            + k[1] * (along_y + beside_y)
            + k[2] * (along_z + at(heat, 7, r, -W))
        )
        qy = (
            k[3] * (along_x + beside_x)
            + k[4] * (t - t_below_y)
            + k[5] * (along_z + at(heat, 7, r, -1))
        )
        qz = (
            k[6] * (at(heat, 5, r, W) - at(heat, 5, r, -W))
            + k[7] * (at(heat, 5, r, 1) - at(heat, 5, r, -1))
            + k[8] * at(heat, 6, r)
        )
        put(heat, 8, r, qx)
        put(heat, 9, r, qy)
        put(heat, 10, r, qz)

    def rate_at(r):
        qz = at(heat, 10, r)
        return (
            (at(heat, 8, r, W) - at(heat, 8, r)) + (at(heat, 9, r, 1) - at(heat, 9, r)) + (up(qz) - qz)
        )

    b = [1.0 / 3.0] * 3 + [(j * j + j - 2.0) / (2.0 * j * (j + 1.0)) for j in range(3, SECTIONS + 1)]
    base_rate = 4.0 / (SUPER_SECTIONS * SUPER_SECTIONS + SUPER_SECTIONS - 2.0)
    scale = (GAMMA_RATIO - 1.0) * SUPER_TIME * base_rate

    def section(j, r):
        rate = rate_at(r)
        if j == 1:
            put(heat, 11, r, rate)
            return at(heat, 0, r) + (b[1] * scale) * rate
        mu = (2.0 * j - 1.0) / j * b[j] / b[j - 1]
        nu = -(j - 1.0) / j * b[j] / b[j - 2]
        if j == 2:
            base = (1.0 - mu) * at(heat, 0, r)
        else:
            base = nu * at(heat, j - 2, r) + (1.0 - mu - nu) * at(heat, 0, r)
        return (
            mu * at(heat, j - 1, r)
            + base
            + (mu * scale) * rate
            - ((1.0 - b[j - 1]) * mu * scale) * at(heat, 11, r)
        )

    for j in range(1, SECTIONS):
        each_block(2 + j, W - 1 - j, FLOWS, heat_fluxes)

        def advance(r, j=j):
            pressure = section(j, r)
            put(heat, j, r, pressure)
            put_temperature(r, pressure * at(cell, 4, r))

        each_block(2 + j, W - 2 - j, ADVANCE, advance)

    each_block(2 + SECTIONS, W - 1 - SECTIONS, FLOWS, heat_fluxes)

    for x in range(OWN):
        r = (PAD + (x + RIM) * W + RIM, OWN)
        pressure_out[x] = section(SECTIONS, r)
        density_out[x] = at(cell, 0, r)
        for c in range(3):
            velocity_out[c, x] = at(cell, 1 + c, r)
            magnetic_out[c, x] = at(face, c, r)


def main_call(before, mid, after, kernel=main_kernel, name="main"):
    def shaped(*shape):
        return jax.ShapeDtypeStruct(shape, jnp.float32)

    block = (OWN, OWN, NZ)
    return pl.pallas_call(
        kernel,
        out_shape=(shaped(*block), shaped(3, *block), shaped(*block), shaped(3, *block)),
        scratch_shapes=[
            pltpu.VMEM((n, ROWS, NZ), jnp.float32) for n in (11, 14, 7, 7, 7, 3, 3, 9, 9, 12)
        ],
        compiler_params=pltpu.CompilerParams(vmem_limit_bytes=40 * 1024 * 1024),
        name=name,
    )(before, mid, after)


def in_vmem(kernel, name, arguments, *shapes):
    spec = pl.BlockSpec(memory_space=pltpu.VMEM)
    results = pl.pallas_call(
        kernel,
        in_specs=[spec] * len(arguments),
        out_specs=[spec] * len(shapes),
        out_shape=[pltpu.VMEM(shape, jnp.float32) for shape in shapes],
        name=name,
    )(*arguments)
    return [pltpu.with_memory_space_constraint(a, pltpu.VMEM) for a in results]


def shift(a, axis, by):
    count = lax.axis_size(axis)
    moved = lax.ppermute(a, axis, [(i, (i + by) % count) for i in range(count)])
    return pltpu.with_memory_space_constraint(moved, pltpu.VMEM)


def local(*arguments):
    packed, sent = (8, OWN * RIM, NZ), (8, SENT, NZ)
    own, to_low, to_high = in_vmem(
        pack_kernel, "pack", arguments, (8, OWN * OWN, NZ), packed, packed
    )
    left = shift(to_high, "gy", 1)
    right = shift(to_low, "gy", -1)
    mid, to_low, to_high = in_vmem(
        widen_kernel, "widen", (own, left, right), (8, MID, NZ), sent, sent
    )
    before = shift(to_high, "gx", 1)
    after = shift(to_low, "gx", -1)
    return main_call(before, mid, after)


def solution(mesh):
    grid = P("gx", "gy", None)
    stacked = P(None, "gx", "gy", None)
    return jax.shard_map(
        local,
        mesh=mesh,
        in_specs=(grid, stacked, grid, stacked),
        out_specs=(grid, stacked, grid, stacked),
        check_vma=False,
    )
```

```python
import jax
import jax.numpy as jnp
from jax import lax
from jax.experimental import pallas as pl
from jax.experimental.pallas import tpu as pltpu
from jax.sharding import PartitionSpec as P

SECTIONS = 4
SUPER_SECTIONS = 8
GAMMA_RATIO = 5.0 / 3.0
TIME_STEP = 0.04
SUPER_TIME = 0.08
DENSITY_FLOOR = 0.5
PRESSURE_FLOOR = 0.1
FIELD_FLOOR = 0.05

OWN = 8
RIM = 2 + SECTIONS
W = OWN + 2 * RIM
NZ = 128
PAD = 32
ROWS = PAD + W * W + 96
SENT = RIM * W
MID = OWN * W
CELLS, COUPLE, FLOWS, ADVANCE = 320, 152, 48, 288


def is_even(axis):
    return lax.axis_index(axis) % 2 == 0


def pack_kernel(mass_ref, velocity_ref, stress_ref, magnetic_ref, own_ref, near_ref, far_ref):
    even = is_even("gy")
    for x in range(OWN):
        fields = [mass_ref[x]] + [velocity_ref[c, x] for c in range(3)]
        fields += [stress_ref[x]] + [magnetic_ref[c, x] for c in range(3)]
        for n, value in enumerate(fields):
            low, high = value[:RIM], value[OWN - RIM :]
            own_ref[n, OWN * x : OWN * (x + 1)] = value
            near_ref[n, RIM * x : RIM * (x + 1)] = jnp.where(even, high, low)
            far_ref[n, RIM * x : RIM * (x + 1)] = jnp.where(even, low, high)


def widen_kernel(own_ref, near_ref, far_ref, mid_ref, sent_ref):
    even = is_even("gy")
    for x in range(OWN):
        for n in range(8):
            near = near_ref[n, RIM * x : RIM * (x + 1)]
            far = far_ref[n, RIM * x : RIM * (x + 1)]
            at = x * W
            mid_ref[n, at : at + RIM] = jnp.where(even, far, near)
            mid_ref[n, at + RIM : at + RIM + OWN] = own_ref[n, OWN * x : OWN * (x + 1)]
            mid_ref[n, at + RIM + OWN : at + W] = jnp.where(even, near, far)
    first = pl.multiple_of(jnp.where(is_even("gx"), 0, MID - SENT), 8)
    for n in range(8):
        sent_ref[n] = mid_ref[n, pl.ds(first, SENT), :]


def up(a):
    return pltpu.roll(a, NZ - 1, 1)


def down(a, by=1):
    return pltpu.roll(a, by, 1)


def half_slope(below, above):
    slope = jnp.minimum(jnp.maximum(below, jnp.minimum(above, 0.0)), jnp.maximum(above, 0.0))
    return 0.5 * slope


def state_terms(state, field, d):
    density, velocity, pressure = state[0], state[1:4], state[4]
    magnetic_sq = field[0] * field[0] + field[1] * field[1] + field[2] * field[2]
    projection = velocity[0] * field[0] + velocity[1] * field[1] + velocity[2] * field[2]
    momentum = [density * velocity[c] for c in range(3)]
    twice_kinetic = (
        momentum[0] * velocity[0] + momentum[1] * velocity[1] + momentum[2] * velocity[2]
    )
    half_sq = 0.5 * magnetic_sq
    total_pressure = pressure + half_sq
    energy = 1.5 * pressure + (0.5 * twice_kinetic + half_sq)
    speed = velocity[d]
    wave_arg = GAMMA_RATIO * pressure + magnetic_sq
    signal = jnp.abs(speed) + wave_arg * lax.rsqrt(wave_arg * density)
    others = [c for c in range(3) if c != d]
    conserved = [density] + momentum + [energy] + [field[c] for c in others]
    carried = [momentum[d]]
    for c in range(3):
        term = momentum[d] * velocity[c]
        carried.append(term + total_pressure if c == d else term)
    carried.append((energy + total_pressure) * speed)
    carried += [speed * field[c] for c in others]
    return conserved, carried, signal, projection


def twice_flux(lower, upper, normal, d):
    others = [c for c in range(3) if c != d]

    def field_of(state):
        field = [normal, normal, normal]
        for at, c in enumerate(others):
            field[c] = state[5 + at]
        return field

    field_low, field_up = field_of(lower), field_of(upper)
    u_low, f_low, s_low, j_low = state_terms(lower, field_low, d)
    u_up, f_up, s_up, j_up = state_terms(upper, field_up, d)
    signal = jnp.maximum(s_low, s_up)
    tension = [None]
    for c in range(3):
        tension.append(field_low[c] + field_up[c])
    tension.append(j_low + j_up)
    tension += [lower[1 + c] + upper[1 + c] for c in others]
    result = []
    for n in range(7):
        central = f_low[n] + f_up[n]
        if tension[n] is not None:
            central = central - normal * tension[n]
        result.append(central - signal * (u_up[n] - u_low[n]))
    return result


def at(ref, n, r, offset=0):
    return ref[n, pl.ds(r[0] + offset, r[1]), :]


def put(ref, n, r, value):
    ref[n, pl.ds(r[0], r[1]), :] = value


def blocks(begin, rows, count, body):
    def step(i, carry):
        body((pl.multiple_of(PAD + begin + i * rows, 8), rows))
        return carry

    if count == 1:
        step(0, 0)
    else:
        lax.fori_loop(0, count, step, 0)


def each_block(first, last, rows, body):
    begin = first * W // 8 * 8
    blocks(begin, rows, -(-(last * W - begin) // rows), body)


def cell_fields(q, r):
    put(q, 8, r, 0.5 * (at(q, 5, r) + at(q, 5, r, W)))
    put(q, 9, r, 0.5 * (at(q, 6, r) + at(q, 6, r, 1)))
    bz = at(q, 7, r)
    put(q, 10, r, 0.5 * (bz + up(bz)))


def changing(d):
    return list(range(5)) + [8 + c for c in range(3) if c != d]


def side_states(q, hi, d, offset, r, n, name):
    value = at(q, name, r)
    half = half_slope(value - at(q, name, r, -offset), at(q, name, r, offset) - value)
    put(hi, n, r, value + half)
    return value - half


def side_fluxes(q, hi, d, offset, target, r):
    upper = [side_states(q, hi, d, offset, r, n, name) for n, name in enumerate(changing(d))]
    lower = [at(hi, n, r, -offset) for n in range(7)]
    for n, value in enumerate(twice_flux(lower, upper, at(q, 5 + d, r), d)):
        put(target, n, r, value)


def stored_states(q, hi, d, offset, r):
    for n, name in enumerate(changing(d)):
        put(hi, 7 + n, r, side_states(q, hi, d, offset, r, n, name))


def stored_fluxes(q, hi, d, offset, target, r):
    upper = [at(hi, 7 + n, r) for n in range(7)]
    lower = [at(hi, n, r, -offset) for n in range(7)]
    for n, value in enumerate(twice_flux(lower, upper, at(q, 5 + d, r), d)):
        put(target, n, r, value)


def height_states(q, hi, r):
    for n, name in enumerate(changing(2)):
        value = at(q, name, r)
        before, earlier, after = down(value), down(value, 2), up(value)
        below = value - before
        put(hi, 7 + n, r, value - half_slope(below, after - value))
        put(hi, n, r, before + half_slope(before - earlier, below))


def early_kernel(mid_ref, near_ref, q, gx, gy, gz, hi):
    even = is_even("gx")
    source = pl.multiple_of(jnp.where(even, 0, MID - SENT), 8)
    target = pl.multiple_of(PAD + jnp.where(even, SENT + MID, 0), 8)
    for n in range(8):
        q[n, PAD + SENT : PAD + SENT + MID] = mid_ref[n]
        q[n, pl.ds(target, SENT), :] = near_ref[n, pl.ds(source, SENT), :]
    base = jnp.where(even, SENT, 0)
    blocks(base, SENT + MID, 1, lambda r: cell_fields(q, r))
    blocks(base, 136, 2, lambda r: height_states(q, hi, r))
    blocks(base, 16, 17, lambda r: stored_fluxes(q, hi, 2, 0, gz, r))
    blocks(base, 16, 17, lambda r: side_fluxes(q, hi, 1, 1, gy, r))
    blocks(base + 16, 16, 16, lambda r: side_fluxes(q, hi, 0, W, gx, r))


def main_kernel(
    far_ref,
    q_in,
    gx_in,
    gy_in,
    gz_in,
    density_out,
    velocity_out,
    pressure_out,
    magnetic_out,
    q,
    gx,
    gy,
    gz,
    hi,
    edge,
    face,
    cell,
    coupling,
    heat,
):
    even = is_even("gx")
    target = pl.multiple_of(PAD + jnp.where(even, 0, SENT + MID), 8)
    for n in range(8):
        q[n, pl.ds(target, SENT), :] = far_ref[n]
    base = jnp.where(even, 0, 256)
    blocks(base, 144, 1, lambda r: cell_fields(q, r))
    blocks(base, 128, 1, lambda r: height_states(q, hi, r))
    blocks(base, 16, 8, lambda r: stored_fluxes(q, hi, 2, 0, gz, r))
    base = jnp.where(even, 0, 240)
    blocks(base, 16, 9, lambda r: side_fluxes(q, hi, 1, 1, gy, r))
    base = jnp.where(even, 16, 232)
    blocks(base, 152, 1, lambda r: stored_states(q, hi, 0, W, r))
    blocks(base + 24, 16, 8, lambda r: stored_fluxes(q, hi, 0, W, gx, r))

    quarter = 0.125 * TIME_STEP

    def edges(r):
        fx_z = at(gx, 6, r)
        fy_z = at(gy, 6, r)
        put(
            edge, 0, r, quarter * (at(gz, 6, r, -1) + at(gz, 6, r) - down(fy_z) - fy_z)
        )
        put(
            edge, 1, r, quarter * (down(fx_z) + fx_z - at(gz, 5, r, -W) - at(gz, 5, r))
        )
        put(
            edge,
            2,
            r,
            quarter * (at(gy, 5, r, -W) + at(gy, 5, r) - at(gx, 5, r, -1) - at(gx, 5, r)),
        )

    each_block(2, W - 1, 344, edges)

    def new_faces(r):
        ex, ey, ez = at(edge, 0, r), at(edge, 1, r), at(edge, 2, r)
        put(face, 0, r, at(q, 5, r) - (at(edge, 2, r, 1) - ez) + (up(ey) - ey))
        put(face, 1, r, at(q, 6, r) - (up(ex) - ex) + (at(edge, 2, r, W) - ez))
        put(face, 2, r, at(q, 7, r) - (at(edge, 1, r, W) - ey) + (at(edge, 0, r, 1) - ex))

    each_block(2, W - 1, 344, new_faces)

    def put_temperature(r, temperature):
        above, below = up(temperature), down(temperature)
        put(heat, 4, r, temperature)
        put(heat, 5, r, temperature + below)
        put(heat, 6, r, temperature - below)
        put(heat, 7, r, above - below)

    def new_cells(r):
        density = at(q, 0, r)
        momentum = [density * at(q, 1 + c, r) for c in range(3)]
        twice_kinetic = (
            momentum[0] * at(q, 1, r) + momentum[1] * at(q, 2, r) + momentum[2] * at(q, 3, r)
        )
        field_sq = (
            at(q, 8, r) * at(q, 8, r) + at(q, 9, r) * at(q, 9, r) + at(q, 10, r) * at(q, 10, r)
        )
        energy = 1.5 * at(q, 4, r) + 0.5 * (twice_kinetic + field_sq)
        updated = []
        for n, value in enumerate([density] + momentum + [energy]):
            change = (at(gx, n, r, W) - at(gx, n, r)) + (at(gy, n, r, 1) - at(gy, n, r))
            above = at(gz, n, r)
            updated.append(value - (0.5 * TIME_STEP) * (change + (up(above) - above)))
        floored = jnp.maximum(updated[0], DENSITY_FLOOR)
        inverse = 1.0 / floored
        velocity = [updated[1 + c] * inverse for c in range(3)]
        bz = at(face, 2, r)
        field = [
            0.5 * (at(face, 0, r) + at(face, 0, r, W)),
            0.5 * (at(face, 1, r) + at(face, 1, r, 1)),
            0.5 * (bz + up(bz)),
        ]
        twice_kinetic = (
            updated[1] * velocity[0] + updated[2] * velocity[1] + updated[3] * velocity[2]
        )
        field_sq = field[0] * field[0] + field[1] * field[1] + field[2] * field[2]
        internal = updated[4] - 0.5 * (twice_kinetic + field_sq)
        pressure = jnp.maximum((GAMMA_RATIO - 1.0) * internal, PRESSURE_FLOOR)
        temperature = pressure * inverse
        put(cell, 0, r, floored)
        for c in range(3):
            put(cell, 1 + c, r, velocity[c])
            put(cell, 6 + c, r, field[c])
        put(cell, 4, r, inverse)
        put(cell, 5, r, temperature * temperature * jnp.sqrt(temperature))
        put(heat, 0, r, pressure)
        put_temperature(r, temperature)

    each_block(2, W - 2, CELLS, new_cells)

    def couple(r):
        own_field = [at(cell, 6 + c, r) for c in range(3)]
        own_conduct = at(cell, 5, r)
        for d in range(3):
            if d < 2:
                offset = -W if d == 0 else -1
                beside = [at(cell, 6 + c, r, offset) for c in range(3)]
                conduct = at(cell, 5, r, offset)
            else:
                beside = [down(a) for a in own_field]
                conduct = down(own_conduct)
            normal = at(face, d, r)
            parts = [normal if c == d else 0.5 * (own_field[c] + beside[c]) for c in range(3)]
            size = parts[0] * parts[0] + parts[1] * parts[1] + parts[2] * parts[2]
            factor = 0.5 * (own_conduct + conduct) / jnp.maximum(size, FIELD_FLOOR) * normal
            mixed = 0.25 * factor
            for c in range(3):
                put(coupling, 3 * d + c, r, (factor if c == d else mixed) * parts[c])

    each_block(3, W - 2, COUPLE, couple)

    def heat_fluxes(r):
        t = at(heat, 4, r)
        t_below_x = at(heat, 4, r, -W)
        t_below_y = at(heat, 4, r, -1)
        along_x = at(heat, 4, r, W) - t_below_x
        along_y = at(heat, 4, r, 1) - t_below_y
        along_z = at(heat, 7, r)
        beside_x = at(heat, 4, r, W - 1) - at(heat, 4, r, -W - 1)
        beside_y = at(heat, 4, r, 1 - W) - at(heat, 4, r, -1 - W)
        k = [at(coupling, n, r) for n in range(9)]
        qx = (
            k[0] * (t - t_below_x)
            + k[1] * (along_y + beside_y)
            + k[2] * (along_z + at(heat, 7, r, -W))
        )
        qy = (
            k[3] * (along_x + beside_x)
            + k[4] * (t - t_below_y)
            + k[5] * (along_z + at(heat, 7, r, -1))
        )
        qz = (
            k[6] * (at(heat, 5, r, W) - at(heat, 5, r, -W))
            + k[7] * (at(heat, 5, r, 1) - at(heat, 5, r, -1))
            + k[8] * at(heat, 6, r)
        )
        put(heat, 8, r, qx)
        put(heat, 9, r, qy)
        put(heat, 10, r, qz)

    def rate_at(r):
        qz = at(heat, 10, r)
        return (
            (at(heat, 8, r, W) - at(heat, 8, r)) + (at(heat, 9, r, 1) - at(heat, 9, r)) + (up(qz) - qz)
        )

    b = [1.0 / 3.0] * 3 + [(j * j + j - 2.0) / (2.0 * j * (j + 1.0)) for j in range(3, SECTIONS + 1)]
    base_rate = 4.0 / (SUPER_SECTIONS * SUPER_SECTIONS + SUPER_SECTIONS - 2.0)
    scale = (GAMMA_RATIO - 1.0) * SUPER_TIME * base_rate

    def section(j, r):
        rate = rate_at(r)
        if j == 1:
            put(heat, 11, r, rate)
            return at(heat, 0, r) + (b[1] * scale) * rate
        mu = (2.0 * j - 1.0) / j * b[j] / b[j - 1]
        nu = -(j - 1.0) / j * b[j] / b[j - 2]
        if j == 2:
            base = (1.0 - mu) * at(heat, 0, r)
        else:
            base = nu * at(heat, j - 2, r) + (1.0 - mu - nu) * at(heat, 0, r)
        return (
            mu * at(heat, j - 1, r)
            + base
            + (mu * scale) * rate
            - ((1.0 - b[j - 1]) * mu * scale) * at(heat, 11, r)
        )

    for j in range(1, SECTIONS):
        each_block(2 + j, W - 1 - j, FLOWS, heat_fluxes)

        def advance(r, j=j):
            pressure = section(j, r)
            put(heat, j, r, pressure)
            put_temperature(r, pressure * at(cell, 4, r))

        each_block(2 + j, W - 2 - j, ADVANCE, advance)

    each_block(2 + SECTIONS, W - 1 - SECTIONS, FLOWS, heat_fluxes)

    for x in range(OWN):
        r = (PAD + (x + RIM) * W + RIM, OWN)
        pressure_out[x] = section(SECTIONS, r)
        density_out[x] = at(cell, 0, r)
        for c in range(3):
            velocity_out[c, x] = at(cell, 1 + c, r)
            magnetic_out[c, x] = at(face, c, r)


def kept(a):
    return pltpu.with_memory_space_constraint(a, pltpu.VMEM)


def in_vmem(*shape):
    return pltpu.VMEM(shape, jnp.float32)


def on_chip(kernel, name, arguments, shapes, scratch=(), limit=None):
    spec = pl.BlockSpec(memory_space=pltpu.VMEM)
    results = pl.pallas_call(
        kernel,
        in_specs=[spec] * len(arguments),
        out_specs=[spec] * len(shapes),
        out_shape=[in_vmem(*shape) for shape in shapes],
        scratch_shapes=[pltpu.VMEM(shape, jnp.float32) for shape in scratch],
        compiler_params=pltpu.CompilerParams(vmem_limit_bytes=limit),
        name=name,
    )(*arguments)
    return [kept(a) for a in results]


def swapped(a, axis, near):
    count = lax.axis_size(axis)
    step = 1 if near else count - 1
    pairs = [(i, (i + (step if i % 2 == 0 else count - step)) % count) for i in range(count)]
    return kept(lax.ppermute(a, axis, pairs))


def main_call(far, buffers):
    spec = pl.BlockSpec(memory_space=pltpu.VMEM)
    block = (OWN, OWN, NZ)
    shapes = (block, (3, *block), block, (3, *block))
    return pl.pallas_call(
        main_kernel,
        in_specs=[spec] * 5,
        out_specs=[spec] * 8,
        out_shape=[jax.ShapeDtypeStruct(shape, jnp.float32) for shape in shapes]
        + [in_vmem(*a.shape) for a in buffers],
        input_output_aliases={1 + n: 4 + n for n in range(4)},
        scratch_shapes=[pltpu.VMEM((n, ROWS, NZ), jnp.float32) for n in (14, 3, 3, 9, 9, 12)],
        compiler_params=pltpu.CompilerParams(vmem_limit_bytes=24 * 1024 * 1024),
        name="main",
    )(far, *buffers)[:4]


def local(*arguments):
    packed = (8, OWN * RIM, NZ)
    own, near, far = on_chip(pack_kernel, "pack", arguments, [(8, OWN * OWN, NZ), packed, packed])
    far = swapped(far, "gy", False)
    near = swapped(near, "gy", True)
    mid, sent = on_chip(widen_kernel, "widen", (own, near, far), [(8, MID, NZ), (8, SENT, NZ)])
    far = swapped(sent, "gx", False)
    near = swapped(mid, "gx", True)
    shapes = [(n, ROWS, NZ) for n in (11, 7, 7, 7)]
    buffers = on_chip(early_kernel, "early", (mid, near), shapes, [(14, ROWS, NZ)], 24 << 20)
    return tuple(main_call(far, buffers))


def solution(mesh):
    grid = P("gx", "gy", None)
    stacked = P(None, "gx", "gy", None)
    return jax.shard_map(
        local,
        mesh=mesh,
        in_specs=(grid, stacked, grid, stacked),
        out_specs=(grid, stacked, grid, stacked),
        check_vma=False,
    )
```

```python
import jax
import jax.numpy as jnp
from jax import lax
from jax.experimental import pallas as pl
from jax.experimental.pallas import tpu as pltpu
from jax.sharding import PartitionSpec as P

SECTIONS = 4
SUPER_SECTIONS = 8
GAMMA_RATIO = 5.0 / 3.0
TIME_STEP = 0.04
SUPER_TIME = 0.08
DENSITY_FLOOR = 0.5
PRESSURE_FLOOR = 0.1
FIELD_FLOOR = 0.05

OWN = 8
RIM = 2 + SECTIONS
W = OWN + 2 * RIM
NZ = 128
PAD = 32
ROWS = PAD + W * W + 96
SENT = RIM * W
MID = OWN * W
FZ, FY, FX, FLOWS, ADVANCE = 16, 16, 16, 48, 288


def is_even(axis):
    return lax.axis_index(axis) % 2 == 0


def pack_kernel(mass_ref, velocity_ref, stress_ref, magnetic_ref, own_ref, near_ref, far_ref):
    even = is_even("gy")
    for x in range(OWN):
        fields = [mass_ref[x]] + [velocity_ref[c, x] for c in range(3)]
        fields += [stress_ref[x]] + [magnetic_ref[c, x] for c in range(3)]
        for n, value in enumerate(fields):
            low, high = value[:RIM], value[OWN - RIM :]
            own_ref[n, OWN * x : OWN * (x + 1)] = value
            near_ref[n, RIM * x : RIM * (x + 1)] = jnp.where(even, high, low)
            far_ref[n, RIM * x : RIM * (x + 1)] = jnp.where(even, low, high)


def widen_kernel(own_ref, near_ref, far_ref, mid_ref, sent_ref):
    even = is_even("gy")
    for x in range(OWN):
        for n in range(8):
            near = near_ref[n, RIM * x : RIM * (x + 1)]
            far = far_ref[n, RIM * x : RIM * (x + 1)]
            at = x * W
            mid_ref[n, at : at + RIM] = jnp.where(even, far, near)
            mid_ref[n, at + RIM : at + RIM + OWN] = own_ref[n, OWN * x : OWN * (x + 1)]
            mid_ref[n, at + RIM + OWN : at + W] = jnp.where(even, near, far)
    first = pl.multiple_of(jnp.where(is_even("gx"), 0, MID - SENT), 8)
    for n in range(8):
        sent_ref[n] = mid_ref[n, pl.ds(first, SENT), :]


def up(a):
    return pltpu.roll(a, NZ - 1, 1)


def down(a, by=1):
    return pltpu.roll(a, by, 1)


def half_slope(below, above):
    slope = jnp.minimum(jnp.maximum(below, jnp.minimum(above, 0.0)), jnp.maximum(above, 0.0))
    return 0.5 * slope


def state_terms(state, field, d):
    density, velocity, pressure = state[0], state[1:4], state[4]
    magnetic_sq = field[0] * field[0] + field[1] * field[1] + field[2] * field[2]
    projection = velocity[0] * field[0] + velocity[1] * field[1] + velocity[2] * field[2]
    momentum = [density * velocity[c] for c in range(3)]
    twice_kinetic = (
        momentum[0] * velocity[0] + momentum[1] * velocity[1] + momentum[2] * velocity[2]
    )
    half_sq = 0.5 * magnetic_sq
    total_pressure = pressure + half_sq
    energy = 1.5 * pressure + (0.5 * twice_kinetic + half_sq)
    speed = velocity[d]
    wave_arg = GAMMA_RATIO * pressure + magnetic_sq
    signal = jnp.abs(speed) + wave_arg * lax.rsqrt(wave_arg * density)
    others = [c for c in range(3) if c != d]
    conserved = [density] + momentum + [energy] + [field[c] for c in others]
    carried = [momentum[d]]
    for c in range(3):
        term = momentum[d] * velocity[c]
        carried.append(term + total_pressure if c == d else term)
    carried.append((energy + total_pressure) * speed)
    carried += [speed * field[c] for c in others]
    return conserved, carried, signal, projection


def twice_flux(lower, upper, normal, d):
    others = [c for c in range(3) if c != d]

    def field_of(state):
        field = [normal, normal, normal]
        for at, c in enumerate(others):
            field[c] = state[5 + at]
        return field

    field_low, field_up = field_of(lower), field_of(upper)
    u_low, f_low, s_low, j_low = state_terms(lower, field_low, d)
    u_up, f_up, s_up, j_up = state_terms(upper, field_up, d)
    signal = jnp.maximum(s_low, s_up)
    tension = [None]
    for c in range(3):
        tension.append(field_low[c] + field_up[c])
    tension.append(j_low + j_up)
    tension += [lower[1 + c] + upper[1 + c] for c in others]
    result = []
    for n in range(7):
        central = f_low[n] + f_up[n]
        if tension[n] is not None:
            central = central - normal * tension[n]
        result.append(central - signal * (u_up[n] - u_low[n]))
    return result


def at(ref, n, r, offset=0):
    return ref[n, pl.ds(r[0] + offset, r[1]), :]


def put(ref, n, r, value):
    ref[n, pl.ds(r[0], r[1]), :] = value


def blocks(begin, rows, count, body):
    def step(i, carry):
        body((pl.multiple_of(PAD + begin + i * rows, 8), rows))
        return carry

    if count == 1:
        step(0, 0)
    else:
        lax.fori_loop(0, count, step, 0)


def each_block(first, last, rows, body):
    begin = first * W // 8 * 8
    blocks(begin, rows, -(-(last * W - begin) // rows), body)


def cell_fields(q, r):
    put(q, 8, r, 0.5 * (at(q, 5, r) + at(q, 5, r, W)))
    put(q, 9, r, 0.5 * (at(q, 6, r) + at(q, 6, r, 1)))
    bz = at(q, 7, r)
    put(q, 10, r, 0.5 * (bz + up(bz)))


def changing(d):
    return list(range(5)) + [8 + c for c in range(3) if c != d]


def side_states(q, hi, d, offset, r, n, name):
    value = at(q, name, r)
    half = half_slope(value - at(q, name, r, -offset), at(q, name, r, offset) - value)
    put(hi, n, r, value + half)
    return value - half


def side_fluxes(q, hi, d, offset, target, r):
    upper = [side_states(q, hi, d, offset, r, n, name) for n, name in enumerate(changing(d))]
    lower = [at(hi, n, r, -offset) for n in range(7)]
    for n, value in enumerate(twice_flux(lower, upper, at(q, 5 + d, r), d)):
        put(target, n, r, value)


def stored_states(q, hi, d, offset, r):
    for n, name in enumerate(changing(d)):
        put(hi, 7 + n, r, side_states(q, hi, d, offset, r, n, name))


def stored_fluxes(q, hi, d, offset, target, r):
    upper = [at(hi, 7 + n, r) for n in range(7)]
    lower = [at(hi, n, r, -offset) for n in range(7)]
    for n, value in enumerate(twice_flux(lower, upper, at(q, 5 + d, r), d)):
        put(target, n, r, value)


def height_states(q, hi, r):
    for n, name in enumerate(changing(2)):
        value = at(q, name, r)
        before, earlier, after = down(value), down(value, 2), up(value)
        below = value - before
        put(hi, 7 + n, r, value - half_slope(below, after - value))
        put(hi, n, r, before + half_slope(before - earlier, below))


QUARTER = 0.125 * TIME_STEP


def edges(gx, gy, gz, edge, r):
    fx_z = at(gx, 6, r)
    fy_z = at(gy, 6, r)
    put(
        edge, 0, r, QUARTER * (at(gz, 6, r, -1) + at(gz, 6, r) - down(fy_z) - fy_z)
    )
    put(
        edge, 1, r, QUARTER * (down(fx_z) + fx_z - at(gz, 5, r, -W) - at(gz, 5, r))
    )
    put(
        edge,
        2,
        r,
        QUARTER * (at(gy, 5, r, -W) + at(gy, 5, r) - at(gx, 5, r, -1) - at(gx, 5, r)),
    )


def new_faces(q, edge, face, r):
    ex, ey, ez = at(edge, 0, r), at(edge, 1, r), at(edge, 2, r)
    put(face, 0, r, at(q, 5, r) - (at(edge, 2, r, 1) - ez) + (up(ey) - ey))
    put(face, 1, r, at(q, 6, r) - (up(ex) - ex) + (at(edge, 2, r, W) - ez))
    put(face, 2, r, at(q, 7, r) - (at(edge, 1, r, W) - ey) + (at(edge, 0, r, 1) - ex))


def put_temperature(heat, r, temperature):
    above, below = up(temperature), down(temperature)
    put(heat, 4, r, temperature)
    put(heat, 5, r, temperature + below)
    put(heat, 6, r, temperature - below)
    put(heat, 7, r, above - below)


def new_cells(q, gx, gy, gz, face, cell, heat, r):
    density = at(q, 0, r)
    momentum = [density * at(q, 1 + c, r) for c in range(3)]
    twice_kinetic = (
        momentum[0] * at(q, 1, r) + momentum[1] * at(q, 2, r) + momentum[2] * at(q, 3, r)
    )
    field_sq = (
        at(q, 8, r) * at(q, 8, r) + at(q, 9, r) * at(q, 9, r) + at(q, 10, r) * at(q, 10, r)
    )
    energy = 1.5 * at(q, 4, r) + 0.5 * (twice_kinetic + field_sq)
    updated = []
    for n, value in enumerate([density] + momentum + [energy]):
        change = (at(gx, n, r, W) - at(gx, n, r)) + (at(gy, n, r, 1) - at(gy, n, r))
        above = at(gz, n, r)
        updated.append(value - (0.5 * TIME_STEP) * (change + (up(above) - above)))
    floored = jnp.maximum(updated[0], DENSITY_FLOOR)
    inverse = 1.0 / floored
    velocity = [updated[1 + c] * inverse for c in range(3)]
    bz = at(face, 2, r)
    field = [
        0.5 * (at(face, 0, r) + at(face, 0, r, W)),
        0.5 * (at(face, 1, r) + at(face, 1, r, 1)),
        0.5 * (bz + up(bz)),
    ]
    twice_kinetic = (
        updated[1] * velocity[0] + updated[2] * velocity[1] + updated[3] * velocity[2]
    )
    field_sq = field[0] * field[0] + field[1] * field[1] + field[2] * field[2]
    internal = updated[4] - 0.5 * (twice_kinetic + field_sq)
    pressure = jnp.maximum((GAMMA_RATIO - 1.0) * internal, PRESSURE_FLOOR)
    temperature = pressure * inverse
    put(cell, 0, r, floored)
    for c in range(3):
        put(cell, 1 + c, r, velocity[c])
        put(cell, 6 + c, r, field[c])
    put(cell, 4, r, inverse)
    put(cell, 5, r, temperature * temperature * jnp.sqrt(temperature))
    put(heat, 0, r, pressure)
    put_temperature(heat, r, temperature)


def couple(face, cell, coupling, r):
    own_field = [at(cell, 6 + c, r) for c in range(3)]
    own_conduct = at(cell, 5, r)
    for d in range(3):
        if d < 2:
            offset = -W if d == 0 else -1
            beside = [at(cell, 6 + c, r, offset) for c in range(3)]
            conduct = at(cell, 5, r, offset)
        else:
            beside = [down(a) for a in own_field]
            conduct = down(own_conduct)
        normal = at(face, d, r)
        parts = [normal if c == d else 0.5 * (own_field[c] + beside[c]) for c in range(3)]
        size = parts[0] * parts[0] + parts[1] * parts[1] + parts[2] * parts[2]
        factor = 0.5 * (own_conduct + conduct) / jnp.maximum(size, FIELD_FLOOR) * normal
        mixed = 0.25 * factor
        for c in range(3):
            put(coupling, 3 * d + c, r, (factor if c == d else mixed) * parts[c])


def early_kernel(mid_ref, near_ref, q, gx, gy, gz, edge, face, cell, coupling, heat, hi):
    even = is_even("gx")
    source = pl.multiple_of(jnp.where(even, 0, MID - SENT), 8)
    target = pl.multiple_of(PAD + jnp.where(even, SENT + MID, 0), 8)
    for n in range(8):
        q[n, PAD + SENT : PAD + SENT + MID] = mid_ref[n]
        q[n, pl.ds(target, SENT), :] = near_ref[n, pl.ds(source, SENT), :]
    base = jnp.where(even, SENT, 0)
    blocks(base, SENT + MID, 1, lambda r: cell_fields(q, r))
    blocks(base, 136, 2, lambda r: height_states(q, hi, r))
    blocks(base, 16, 17, lambda r: stored_fluxes(q, hi, 2, 0, gz, r))
    blocks(base, 16, 17, lambda r: side_fluxes(q, hi, 1, 1, gy, r))
    blocks(base + 16, 16, 16, lambda r: side_fluxes(q, hi, 0, W, gx, r))
    blocks(base + 40, 224, 1, lambda r: edges(gx, gy, gz, edge, r))
    blocks(base + 40, 224, 1, lambda r: new_faces(q, edge, face, r))
    blocks(base + 40, 200, 1, lambda r: new_cells(q, gx, gy, gz, face, cell, heat, r))
    blocks(base + 56, 184, 1, lambda r: couple(face, cell, coupling, r))


def main_kernel(far_ref, *refs):
    density_out, velocity_out, pressure_out, magnetic_out = refs[9:13]
    q, gx, gy, gz, edge, face, cell, coupling, heat, hi = refs[13:]
    even = is_even("gx")
    target = pl.multiple_of(PAD + jnp.where(even, 0, SENT + MID), 8)
    for n in range(8):
        q[n, pl.ds(target, SENT), :] = far_ref[n]

    def begin(of_even, of_odd):
        return jnp.where(even, of_even, of_odd)

    blocks(begin(0, 256), 144, 1, lambda r: cell_fields(q, r))
    blocks(begin(0, 256), 128, 1, lambda r: height_states(q, hi, r))
    blocks(begin(0, 256), FZ, 128 // FZ, lambda r: stored_fluxes(q, hi, 2, 0, gz, r))
    blocks(begin(0, 240), FY, 144 // FY, lambda r: side_fluxes(q, hi, 1, 1, gy, r))
    blocks(begin(16, 232), 152, 1, lambda r: stored_states(q, hi, 0, W, r))
    blocks(begin(40, 256), FX, 128 // FX, lambda r: stored_fluxes(q, hi, 0, W, gx, r))
    blocks(begin(40, 256), 128, 1, lambda r: edges(gx, gy, gz, edge, r))
    blocks(begin(40, 240), 144, 1, lambda r: new_faces(q, edge, face, r))
    blocks(begin(40, 240), 120, 1, lambda r: new_cells(q, gx, gy, gz, face, cell, heat, r))
    blocks(begin(56, 240), 128, 1, lambda r: couple(face, cell, coupling, r))

    def heat_fluxes(r):
        t = at(heat, 4, r)
        t_below_x = at(heat, 4, r, -W)
        t_below_y = at(heat, 4, r, -1)
        along_x = at(heat, 4, r, W) - t_below_x
        along_y = at(heat, 4, r, 1) - t_below_y
        along_z = at(heat, 7, r)
        beside_x = at(heat, 4, r, W - 1) - at(heat, 4, r, -W - 1)
        beside_y = at(heat, 4, r, 1 - W) - at(heat, 4, r, -1 - W)
        k = [at(coupling, n, r) for n in range(9)]
        qx = (
            k[0] * (t - t_below_x)
            + k[1] * (along_y + beside_y)
            + k[2] * (along_z + at(heat, 7, r, -W))
        )
        qy = (
            k[3] * (along_x + beside_x)
            + k[4] * (t - t_below_y)
            + k[5] * (along_z + at(heat, 7, r, -1))
        )
        qz = (
            k[6] * (at(heat, 5, r, W) - at(heat, 5, r, -W))
            + k[7] * (at(heat, 5, r, 1) - at(heat, 5, r, -1))
            + k[8] * at(heat, 6, r)
        )
        put(heat, 8, r, qx)
        put(heat, 9, r, qy)
        put(heat, 10, r, qz)

    def rate_at(r):
        qz = at(heat, 10, r)
        return (
            (at(heat, 8, r, W) - at(heat, 8, r)) + (at(heat, 9, r, 1) - at(heat, 9, r)) + (up(qz) - qz)
        )

    b = [1.0 / 3.0] * 3 + [(j * j + j - 2.0) / (2.0 * j * (j + 1.0)) for j in range(3, SECTIONS + 1)]
    base_rate = 4.0 / (SUPER_SECTIONS * SUPER_SECTIONS + SUPER_SECTIONS - 2.0)
    scale = (GAMMA_RATIO - 1.0) * SUPER_TIME * base_rate

    def section(j, r):
        rate = rate_at(r)
        if j == 1:
            put(heat, 11, r, rate)
            return at(heat, 0, r) + (b[1] * scale) * rate
        mu = (2.0 * j - 1.0) / j * b[j] / b[j - 1]
        nu = -(j - 1.0) / j * b[j] / b[j - 2]
        if j == 2:
            base = (1.0 - mu) * at(heat, 0, r)
        else:
            base = nu * at(heat, j - 2, r) + (1.0 - mu - nu) * at(heat, 0, r)
        return (
            mu * at(heat, j - 1, r)
            + base
            + (mu * scale) * rate
            - ((1.0 - b[j - 1]) * mu * scale) * at(heat, 11, r)
        )

    for j in range(1, SECTIONS):
        each_block(2 + j, W - 1 - j, FLOWS, heat_fluxes)

        def advance(r, j=j):
            pressure = section(j, r)
            put(heat, j, r, pressure)
            put_temperature(heat, r, pressure * at(cell, 4, r))

        each_block(2 + j, W - 2 - j, ADVANCE, advance)

    each_block(2 + SECTIONS, W - 1 - SECTIONS, FLOWS, heat_fluxes)

    for x in range(OWN):
        r = (PAD + (x + RIM) * W + RIM, OWN)
        pressure_out[x] = section(SECTIONS, r)
        density_out[x] = at(cell, 0, r)
        for c in range(3):
            velocity_out[c, x] = at(cell, 1 + c, r)
            magnetic_out[c, x] = at(face, c, r)


def kept(a):
    return pltpu.with_memory_space_constraint(a, pltpu.VMEM)


def in_vmem(*shape):
    return pltpu.VMEM(shape, jnp.float32)


def on_chip(kernel, name, arguments, shapes, scratch=(), limit=None):
    spec = pl.BlockSpec(memory_space=pltpu.VMEM)
    results = pl.pallas_call(
        kernel,
        in_specs=[spec] * len(arguments),
        out_specs=[spec] * len(shapes),
        out_shape=[in_vmem(*shape) for shape in shapes],
        scratch_shapes=[pltpu.VMEM(shape, jnp.float32) for shape in scratch],
        compiler_params=pltpu.CompilerParams(vmem_limit_bytes=limit),
        name=name,
    )(*arguments)
    return [kept(a) for a in results]


def swapped(a, axis, near):
    count = lax.axis_size(axis)
    step = 1 if near else count - 1
    pairs = [(i, (i + (step if i % 2 == 0 else count - step)) % count) for i in range(count)]
    return kept(lax.ppermute(a, axis, pairs))


def main_call(far, buffers):
    spec = pl.BlockSpec(memory_space=pltpu.VMEM)
    block = (OWN, OWN, NZ)
    shapes = (block, (3, *block), block, (3, *block))
    return pl.pallas_call(
        main_kernel,
        in_specs=[spec] * (1 + len(buffers)),
        out_specs=[spec] * (4 + len(buffers)),
        out_shape=[jax.ShapeDtypeStruct(shape, jnp.float32) for shape in shapes]
        + [in_vmem(*a.shape) for a in buffers],
        input_output_aliases={1 + n: 4 + n for n in range(len(buffers))},
        scratch_shapes=[pltpu.VMEM((14, ROWS, NZ), jnp.float32)],
        compiler_params=pltpu.CompilerParams(vmem_limit_bytes=16 << 20),
        name="main",
    )(far, *buffers)[:4]


def local(*arguments):
    packed = (8, OWN * RIM, NZ)
    own, near, far = on_chip(pack_kernel, "pack", arguments, [(8, OWN * OWN, NZ), packed, packed])
    far = swapped(far, "gy", False)
    near = swapped(near, "gy", True)
    mid, sent = on_chip(widen_kernel, "widen", (own, near, far), [(8, MID, NZ), (8, SENT, NZ)])
    far = swapped(sent, "gx", False)
    near = swapped(mid, "gx", True)
    shapes = [(n, ROWS, NZ) for n in (11, 7, 7, 7, 3, 3, 9, 9, 12)]
    buffers = on_chip(early_kernel, "early", (mid, near), shapes, [(14, ROWS, NZ)], 16 << 20)
    return tuple(main_call(far, buffers))


def solution(mesh):
    grid = P("gx", "gy", None)
    stacked = P(None, "gx", "gy", None)
    return jax.shard_map(
        local,
        mesh=mesh,
        in_specs=(grid, stacked, grid, stacked),
        out_specs=(grid, stacked, grid, stacked),
        check_vma=False,
    )
```

```python
import jax
import jax.numpy as jnp
from jax import lax
from jax.experimental import pallas as pl
from jax.experimental.pallas import tpu as pltpu
from jax.sharding import PartitionSpec as P

SECTIONS = 4
SUPER_SECTIONS = 8
GAMMA_RATIO = 5.0 / 3.0
TIME_STEP = 0.04
SUPER_TIME = 0.08
DENSITY_FLOOR = 0.5
PRESSURE_FLOOR = 0.1
FIELD_FLOOR = 0.05

OWN = 8
RIM = 2 + SECTIONS
W = OWN + 2 * RIM
NZ = 128
PAD = 32
ROWS = PAD + W * W + 96
SENT = RIM * W
MID = OWN * W
FZ, FY, FX, FLOWS, ADVANCE = 32, 48, 32, 304, 288


def is_even(axis):
    return lax.axis_index(axis) % 2 == 0


def pack_kernel(mass_ref, velocity_ref, stress_ref, magnetic_ref, own_ref, near_ref, far_ref):
    even = is_even("gy")
    for x in range(OWN):
        fields = [mass_ref[x]] + [velocity_ref[c, x] for c in range(3)]
        fields += [stress_ref[x]] + [magnetic_ref[c, x] for c in range(3)]
        for n, value in enumerate(fields):
            low, high = value[:RIM], value[OWN - RIM :]
            own_ref[n, OWN * x : OWN * (x + 1)] = value
            near_ref[n, RIM * x : RIM * (x + 1)] = jnp.where(even, high, low)
            far_ref[n, RIM * x : RIM * (x + 1)] = jnp.where(even, low, high)


def widen_kernel(own_ref, near_ref, far_ref, mid_ref, sent_ref):
    even = is_even("gy")
    for x in range(OWN):
        for n in range(8):
            near = near_ref[n, RIM * x : RIM * (x + 1)]
            far = far_ref[n, RIM * x : RIM * (x + 1)]
            at = x * W
            mid_ref[n, at : at + RIM] = jnp.where(even, far, near)
            mid_ref[n, at + RIM : at + RIM + OWN] = own_ref[n, OWN * x : OWN * (x + 1)]
            mid_ref[n, at + RIM + OWN : at + W] = jnp.where(even, near, far)
    first = pl.multiple_of(jnp.where(is_even("gx"), 0, MID - SENT), 8)
    for n in range(8):
        sent_ref[n] = mid_ref[n, pl.ds(first, SENT), :]


def up(a):
    return pltpu.roll(a, NZ - 1, 1)


def down(a, by=1):
    return pltpu.roll(a, by, 1)


def half_slope(below, above):
    slope = jnp.minimum(jnp.maximum(below, jnp.minimum(above, 0.0)), jnp.maximum(above, 0.0))
    return 0.5 * slope


def state_terms(state, field, d):
    density, velocity, pressure = state[0], state[1:4], state[4]
    magnetic_sq = field[0] * field[0] + field[1] * field[1] + field[2] * field[2]
    projection = velocity[0] * field[0] + velocity[1] * field[1] + velocity[2] * field[2]
    momentum = [density * velocity[c] for c in range(3)]
    twice_kinetic = (
        momentum[0] * velocity[0] + momentum[1] * velocity[1] + momentum[2] * velocity[2]
    )
    half_sq = 0.5 * magnetic_sq
    total_pressure = pressure + half_sq
    energy = 1.5 * pressure + (0.5 * twice_kinetic + half_sq)
    speed = velocity[d]
    wave_arg = GAMMA_RATIO * pressure + magnetic_sq
    signal = jnp.abs(speed) + wave_arg * lax.rsqrt(wave_arg * density)
    others = [c for c in range(3) if c != d]
    conserved = [density] + momentum + [energy] + [field[c] for c in others]
    carried = [momentum[d]]
    for c in range(3):
        term = momentum[d] * velocity[c]
        carried.append(term + total_pressure if c == d else term)
    carried.append((energy + total_pressure) * speed)
    carried += [speed * field[c] for c in others]
    return conserved, carried, signal, projection


def twice_flux(lower, upper, normal, d):
    others = [c for c in range(3) if c != d]

    def field_of(state):
        field = [normal, normal, normal]
        for at, c in enumerate(others):
            field[c] = state[5 + at]
        return field

    field_low, field_up = field_of(lower), field_of(upper)
    u_low, f_low, s_low, j_low = state_terms(lower, field_low, d)
    u_up, f_up, s_up, j_up = state_terms(upper, field_up, d)
    signal = jnp.maximum(s_low, s_up)
    tension = [None]
    for c in range(3):
        tension.append(field_low[c] + field_up[c])
    tension.append(j_low + j_up)
    tension += [lower[1 + c] + upper[1 + c] for c in others]
    result = []
    for n in range(7):
        central = f_low[n] + f_up[n]
        if tension[n] is not None:
            central = central - normal * tension[n]
        result.append(central - signal * (u_up[n] - u_low[n]))
    return result


def at(ref, n, r, offset=0):
    return ref[n, pl.ds(r[0] + offset, r[1]), :]


def put(ref, n, r, value):
    ref[n, pl.ds(r[0], r[1]), :] = value


def blocks(begin, rows, count, body):
    def step(i, carry):
        body((pl.multiple_of(PAD + begin + i * rows, 8), rows))
        return carry

    if count == 1:
        step(0, 0)
    else:
        lax.fori_loop(0, count, step, 0)


def each_block(first, last, rows, body):
    begin = first * W // 8 * 8
    blocks(begin, rows, -(-(last * W - begin) // rows), body)


def cell_fields(q, r):
    put(q, 8, r, 0.5 * (at(q, 5, r) + at(q, 5, r, W)))
    put(q, 9, r, 0.5 * (at(q, 6, r) + at(q, 6, r, 1)))
    bz = at(q, 7, r)
    put(q, 10, r, 0.5 * (bz + up(bz)))


def changing(d):
    return list(range(5)) + [8 + c for c in range(3) if c != d]


def side_states(q, hi, d, offset, r, n, name):
    value = at(q, name, r)
    half = half_slope(value - at(q, name, r, -offset), at(q, name, r, offset) - value)
    put(hi, n, r, value + half)
    return value - half


def side_fluxes(q, hi, d, offset, target, r):
    upper = [side_states(q, hi, d, offset, r, n, name) for n, name in enumerate(changing(d))]
    lower = [at(hi, n, r, -offset) for n in range(7)]
    for n, value in enumerate(twice_flux(lower, upper, at(q, 5 + d, r), d)):
        put(target, n, r, value)


def stored_states(q, hi, d, offset, r):
    for n, name in enumerate(changing(d)):
        put(hi, 7 + n, r, side_states(q, hi, d, offset, r, n, name))


def stored_fluxes(q, hi, d, offset, target, r):
    upper = [at(hi, 7 + n, r) for n in range(7)]
    lower = [at(hi, n, r, -offset) for n in range(7)]
    for n, value in enumerate(twice_flux(lower, upper, at(q, 5 + d, r), d)):
        put(target, n, r, value)


def height_states(q, hi, r):
    for n, name in enumerate(changing(2)):
        value = at(q, name, r)
        before, earlier, after = down(value), down(value, 2), up(value)
        below = value - before
        put(hi, 7 + n, r, value - half_slope(below, after - value))
        put(hi, n, r, before + half_slope(before - earlier, below))


QUARTER = 0.125 * TIME_STEP


def edges(gx, gy, gz, edge, r):
    fx_z = at(gx, 6, r)
    fy_z = at(gy, 6, r)
    put(
        edge, 0, r, QUARTER * (at(gz, 6, r, -1) + at(gz, 6, r) - down(fy_z) - fy_z)
    )
    put(
        edge, 1, r, QUARTER * (down(fx_z) + fx_z - at(gz, 5, r, -W) - at(gz, 5, r))
    )
    put(
        edge,
        2,
        r,
        QUARTER * (at(gy, 5, r, -W) + at(gy, 5, r) - at(gx, 5, r, -1) - at(gx, 5, r)),
    )


def new_faces(q, edge, face, r):
    ex, ey, ez = at(edge, 0, r), at(edge, 1, r), at(edge, 2, r)
    put(face, 0, r, at(q, 5, r) - (at(edge, 2, r, 1) - ez) + (up(ey) - ey))
    put(face, 1, r, at(q, 6, r) - (up(ex) - ex) + (at(edge, 2, r, W) - ez))
    put(face, 2, r, at(q, 7, r) - (at(edge, 1, r, W) - ey) + (at(edge, 0, r, 1) - ex))


def put_temperature(heat, r, temperature):
    above, below = up(temperature), down(temperature)
    put(heat, 4, r, temperature)
    put(heat, 5, r, temperature + below)
    put(heat, 6, r, temperature - below)
    put(heat, 7, r, above - below)


def new_cells(q, gx, gy, gz, face, cell, heat, r):
    density = at(q, 0, r)
    momentum = [density * at(q, 1 + c, r) for c in range(3)]
    twice_kinetic = (
        momentum[0] * at(q, 1, r) + momentum[1] * at(q, 2, r) + momentum[2] * at(q, 3, r)
    )
    field_sq = (
        at(q, 8, r) * at(q, 8, r) + at(q, 9, r) * at(q, 9, r) + at(q, 10, r) * at(q, 10, r)
    )
    energy = 1.5 * at(q, 4, r) + 0.5 * (twice_kinetic + field_sq)
    updated = []
    for n, value in enumerate([density] + momentum + [energy]):
        change = (at(gx, n, r, W) - at(gx, n, r)) + (at(gy, n, r, 1) - at(gy, n, r))
        above = at(gz, n, r)
        updated.append(value - (0.5 * TIME_STEP) * (change + (up(above) - above)))
    floored = jnp.maximum(updated[0], DENSITY_FLOOR)
    inverse = 1.0 / floored
    velocity = [updated[1 + c] * inverse for c in range(3)]
    bz = at(face, 2, r)
    field = [
        0.5 * (at(face, 0, r) + at(face, 0, r, W)),
        0.5 * (at(face, 1, r) + at(face, 1, r, 1)),
        0.5 * (bz + up(bz)),
    ]
    twice_kinetic = (
        updated[1] * velocity[0] + updated[2] * velocity[1] + updated[3] * velocity[2]
    )
    field_sq = field[0] * field[0] + field[1] * field[1] + field[2] * field[2]
    internal = updated[4] - 0.5 * (twice_kinetic + field_sq)
    pressure = jnp.maximum((GAMMA_RATIO - 1.0) * internal, PRESSURE_FLOOR)
    temperature = pressure * inverse
    put(cell, 0, r, floored)
    for c in range(3):
        put(cell, 1 + c, r, velocity[c])
        put(cell, 6 + c, r, field[c])
    put(cell, 4, r, inverse)
    put(cell, 5, r, temperature * temperature * jnp.sqrt(temperature))
    put(heat, 0, r, pressure)
    put_temperature(heat, r, temperature)


def couple(face, cell, coupling, r):
    own_field = [at(cell, 6 + c, r) for c in range(3)]
    own_conduct = at(cell, 5, r)
    for d in range(3):
        if d < 2:
            offset = -W if d == 0 else -1
            beside = [at(cell, 6 + c, r, offset) for c in range(3)]
            conduct = at(cell, 5, r, offset)
        else:
            beside = [down(a) for a in own_field]
            conduct = down(own_conduct)
        normal = at(face, d, r)
        parts = [normal if c == d else 0.5 * (own_field[c] + beside[c]) for c in range(3)]
        size = parts[0] * parts[0] + parts[1] * parts[1] + parts[2] * parts[2]
        factor = 0.5 * (own_conduct + conduct) / jnp.maximum(size, FIELD_FLOOR) * normal
        mixed = 0.25 * factor
        for c in range(3):
            put(coupling, 3 * d + c, r, (factor if c == d else mixed) * parts[c])


def early_kernel(mid_ref, near_ref, q, gx, gy, gz, edge, face, cell, coupling, heat, hi):
    even = is_even("gx")
    source = pl.multiple_of(jnp.where(even, 0, MID - SENT), 8)
    target = pl.multiple_of(PAD + jnp.where(even, SENT + MID, 0), 8)
    for n in range(8):
        q[n, PAD + SENT : PAD + SENT + MID] = mid_ref[n]
        q[n, pl.ds(target, SENT), :] = near_ref[n, pl.ds(source, SENT), :]
    base = jnp.where(even, SENT, 0)
    blocks(base, SENT + MID, 1, lambda r: cell_fields(q, r))
    blocks(base, 136, 2, lambda r: height_states(q, hi, r))
    blocks(base, 16, 17, lambda r: stored_fluxes(q, hi, 2, 0, gz, r))
    blocks(base, 16, 17, lambda r: side_fluxes(q, hi, 1, 1, gy, r))
    blocks(base + 16, 16, 16, lambda r: side_fluxes(q, hi, 0, W, gx, r))
    blocks(base + 40, 224, 1, lambda r: edges(gx, gy, gz, edge, r))
    blocks(base + 40, 224, 1, lambda r: new_faces(q, edge, face, r))
    blocks(base + 40, 200, 1, lambda r: new_cells(q, gx, gy, gz, face, cell, heat, r))
    blocks(base + 56, 184, 1, lambda r: couple(face, cell, coupling, r))


def main_kernel(far_ref, *refs):
    density_out, velocity_out, pressure_out, magnetic_out = refs[9:13]
    q, gx, gy, gz, edge, face, cell, coupling, heat, hi = refs[13:]
    even = is_even("gx")
    target = pl.multiple_of(PAD + jnp.where(even, 0, SENT + MID), 8)
    for n in range(8):
        q[n, pl.ds(target, SENT), :] = far_ref[n]

    def begin(of_even, of_odd):
        return jnp.where(even, of_even, of_odd)

    blocks(begin(0, 256), 144, 1, lambda r: cell_fields(q, r))
    blocks(begin(0, 256), 128, 1, lambda r: height_states(q, hi, r))
    blocks(begin(0, 256), FZ, 128 // FZ, lambda r: stored_fluxes(q, hi, 2, 0, gz, r))
    blocks(begin(0, 240), FY, 144 // FY, lambda r: side_fluxes(q, hi, 1, 1, gy, r))
    blocks(begin(16, 232), 152, 1, lambda r: stored_states(q, hi, 0, W, r))
    blocks(begin(40, 256), FX, 128 // FX, lambda r: stored_fluxes(q, hi, 0, W, gx, r))
    blocks(begin(40, 256), 128, 1, lambda r: edges(gx, gy, gz, edge, r))
    blocks(begin(40, 240), 144, 1, lambda r: new_faces(q, edge, face, r))
    blocks(begin(40, 240), 120, 1, lambda r: new_cells(q, gx, gy, gz, face, cell, heat, r))
    blocks(begin(56, 240), 128, 1, lambda r: couple(face, cell, coupling, r))

    def heat_fluxes(r):
        t = at(heat, 4, r)
        t_below_x = at(heat, 4, r, -W)
        t_below_y = at(heat, 4, r, -1)
        along_x = at(heat, 4, r, W) - t_below_x
        along_y = at(heat, 4, r, 1) - t_below_y
        along_z = at(heat, 7, r)
        beside_x = at(heat, 4, r, W - 1) - at(heat, 4, r, -W - 1)
        beside_y = at(heat, 4, r, 1 - W) - at(heat, 4, r, -1 - W)
        k = [at(coupling, n, r) for n in range(9)]
        qx = (
            k[0] * (t - t_below_x)
            + k[1] * (along_y + beside_y)
            + k[2] * (along_z + at(heat, 7, r, -W))
        )
        qy = (
            k[3] * (along_x + beside_x)
            + k[4] * (t - t_below_y)
            + k[5] * (along_z + at(heat, 7, r, -1))
        )
        qz = (
            k[6] * (at(heat, 5, r, W) - at(heat, 5, r, -W))
            + k[7] * (at(heat, 5, r, 1) - at(heat, 5, r, -1))
            + k[8] * at(heat, 6, r)
        )
        put(heat, 8, r, qx)
        put(heat, 9, r, qy)
        put(heat, 10, r, qz)

    def rate_at(r):
        qz = at(heat, 10, r)
        return (
            (at(heat, 8, r, W) - at(heat, 8, r)) + (at(heat, 9, r, 1) - at(heat, 9, r)) + (up(qz) - qz)
        )

    b = [1.0 / 3.0] * 3 + [(j * j + j - 2.0) / (2.0 * j * (j + 1.0)) for j in range(3, SECTIONS + 1)]
    base_rate = 4.0 / (SUPER_SECTIONS * SUPER_SECTIONS + SUPER_SECTIONS - 2.0)
    scale = (GAMMA_RATIO - 1.0) * SUPER_TIME * base_rate

    def section(j, r):
        rate = rate_at(r)
        if j == 1:
            put(heat, 11, r, rate)
            return at(heat, 0, r) + (b[1] * scale) * rate
        mu = (2.0 * j - 1.0) / j * b[j] / b[j - 1]
        nu = -(j - 1.0) / j * b[j] / b[j - 2]
        if j == 2:
            base = (1.0 - mu) * at(heat, 0, r)
        else:
            base = nu * at(heat, j - 2, r) + (1.0 - mu - nu) * at(heat, 0, r)
        return (
            mu * at(heat, j - 1, r)
            + base
            + (mu * scale) * rate
            - ((1.0 - b[j - 1]) * mu * scale) * at(heat, 11, r)
        )

    for j in range(1, SECTIONS):
        each_block(2 + j, W - 1 - j, FLOWS, heat_fluxes)

        def advance(r, j=j):
            pressure = section(j, r)
            put(heat, j, r, pressure)
            put_temperature(heat, r, pressure * at(cell, 4, r))

        each_block(2 + j, W - 2 - j, ADVANCE, advance)

    each_block(2 + SECTIONS, W - 1 - SECTIONS, FLOWS, heat_fluxes)

    for x in range(OWN):
        r = (PAD + (x + RIM) * W + RIM, OWN)
        pressure_out[x] = section(SECTIONS, r)
        density_out[x] = at(cell, 0, r)
        for c in range(3):
            velocity_out[c, x] = at(cell, 1 + c, r)
            magnetic_out[c, x] = at(face, c, r)


def kept(a):
    return pltpu.with_memory_space_constraint(a, pltpu.VMEM)


def in_vmem(*shape):
    return pltpu.VMEM(shape, jnp.float32)


def on_chip(kernel, name, arguments, shapes, scratch=(), limit=None, cost=None):
    spec = pl.BlockSpec(memory_space=pltpu.VMEM)
    results = pl.pallas_call(
        kernel,
        in_specs=[spec] * len(arguments),
        out_specs=[spec] * len(shapes),
        out_shape=[in_vmem(*shape) for shape in shapes],
        scratch_shapes=[pltpu.VMEM(shape, jnp.float32) for shape in scratch],
        compiler_params=pltpu.CompilerParams(vmem_limit_bytes=limit),
        cost_estimate=cost,
        name=name,
    )(*arguments)
    return [kept(a) for a in results]


def swapped(a, axis, near):
    count = lax.axis_size(axis)
    step = 1 if near else count - 1
    pairs = [(i, (i + (step if i % 2 == 0 else count - step)) % count) for i in range(count)]
    return kept(lax.ppermute(a, axis, pairs))


def main_call(far, buffers):
    spec = pl.BlockSpec(memory_space=pltpu.VMEM)
    block = (OWN, OWN, NZ)
    shapes = (block, (3, *block), block, (3, *block))
    return pl.pallas_call(
        main_kernel,
        in_specs=[spec] * (1 + len(buffers)),
        out_specs=[spec] * (4 + len(buffers)),
        out_shape=[jax.ShapeDtypeStruct(shape, jnp.float32) for shape in shapes]
        + [in_vmem(*a.shape) for a in buffers],
        input_output_aliases={1 + n: 4 + n for n in range(len(buffers))},
        scratch_shapes=[pltpu.VMEM((14, ROWS, NZ), jnp.float32)],
        compiler_params=pltpu.CompilerParams(vmem_limit_bytes=16 << 20),
        name="main",
    )(far, *buffers)[:4]


def local(*arguments):
    packed = (8, OWN * RIM, NZ)
    own, near, far = on_chip(pack_kernel, "pack", arguments, [(8, OWN * OWN, NZ), packed, packed])
    far = swapped(far, "gy", False)
    near = swapped(near, "gy", True)
    mid, sent = on_chip(widen_kernel, "widen", (own, near, far), [(8, MID, NZ), (8, SENT, NZ)])
    far = swapped(sent, "gx", False)
    near = lax.cond(
        lax.axis_index("gx") >= 0, lambda a: swapped(a, "gx", True), lambda a: a, mid
    )
    near = kept(near)
    shapes = [(n, ROWS, NZ) for n in (11, 7, 7, 7, 3, 3, 9, 9, 12)]
    buffers = on_chip(early_kernel, "early", (mid, near), shapes, [(14, ROWS, NZ)], 16 << 20, pl.CostEstimate(flops=0, bytes_accessed=1024, transcendentals=0))
    return tuple(main_call(far, buffers))


def solution(mesh):
    grid = P("gx", "gy", None)
    stacked = P(None, "gx", "gy", None)
    return jax.shard_map(
        local,
        mesh=mesh,
        in_specs=(grid, stacked, grid, stacked),
        out_specs=(grid, stacked, grid, stacked),
        check_vma=False,
    )
```

```python
import jax
import jax.numpy as jnp
from jax import lax
from jax.experimental import pallas as pl
from jax.experimental.pallas import tpu as pltpu
from jax.sharding import PartitionSpec as P

SECTIONS = 4
SUPER_SECTIONS = 8
GAMMA_RATIO = 5.0 / 3.0
TIME_STEP = 0.04
SUPER_TIME = 0.08
DENSITY_FLOOR = 0.5
PRESSURE_FLOOR = 0.1
FIELD_FLOOR = 0.05

OWN = 8
RIM = 2 + SECTIONS
W = OWN + 2 * RIM
NZ = 128
PAD = 32
ROWS = PAD + W * W + 96
SENT = RIM * W
MID = OWN * W
FZ, FY, FX, FLOWS, ADVANCE = 32, 48, 32, 304, 288


def is_even(axis):
    return lax.axis_index(axis) % 2 == 0


def pack_kernel(mass_ref, velocity_ref, stress_ref, magnetic_ref, own_ref, near_ref, far_ref):
    for x in range(OWN):
        fields = [mass_ref[x]] + [velocity_ref[c, x] for c in range(3)]
        fields += [stress_ref[x]] + [magnetic_ref[c, x] for c in range(3)]
        for n, value in enumerate(fields):
            low, high = value[:RIM], value[OWN - RIM :]
            own_ref[n, OWN * x : OWN * (x + 1)] = value
            near_ref[n, RIM * x : RIM * (x + 1)] = high
            far_ref[n, RIM * x : RIM * (x + 1)] = low


def widen_kernel(own_ref, near_ref, far_ref, mid_ref, sent_ref, beside_ref):
    for x in range(OWN):
        for n in range(8):
            near = near_ref[n, RIM * x : RIM * (x + 1)]
            far = far_ref[n, RIM * x : RIM * (x + 1)]
            at = x * W
            mid_ref[n, at : at + RIM] = near
            mid_ref[n, at + RIM : at + RIM + OWN] = own_ref[n, OWN * x : OWN * (x + 1)]
            mid_ref[n, at + RIM + OWN : at + W] = far
    low = pl.multiple_of(jnp.where(is_even("gx"), 0, MID - SENT), 8)
    high = pl.multiple_of(jnp.where(is_even("gx"), MID - SENT, 0), 8)
    for n in range(8):
        sent_ref[n] = mid_ref[n, pl.ds(low, SENT), :]
        beside_ref[n] = mid_ref[n, pl.ds(high, SENT), :]


def up(a):
    return pltpu.roll(a, NZ - 1, 1)


def down(a, by=1):
    return pltpu.roll(a, by, 1)


def half_slope(below, above):
    slope = jnp.minimum(jnp.maximum(below, jnp.minimum(above, 0.0)), jnp.maximum(above, 0.0))
    return 0.5 * slope


def state_terms(state, field, d):
    density, velocity, pressure = state[0], state[1:4], state[4]
    magnetic_sq = field[0] * field[0] + field[1] * field[1] + field[2] * field[2]
    projection = velocity[0] * field[0] + velocity[1] * field[1] + velocity[2] * field[2]
    momentum = [density * velocity[c] for c in range(3)]
    twice_kinetic = (
        momentum[0] * velocity[0] + momentum[1] * velocity[1] + momentum[2] * velocity[2]
    )
    half_sq = 0.5 * magnetic_sq
    total_pressure = pressure + half_sq
    energy = 1.5 * pressure + (0.5 * twice_kinetic + half_sq)
    speed = velocity[d]
    wave_arg = GAMMA_RATIO * pressure + magnetic_sq
    signal = jnp.abs(speed) + wave_arg * lax.rsqrt(wave_arg * density)
    others = [c for c in range(3) if c != d]
    conserved = [density] + momentum + [energy] + [field[c] for c in others]
    carried = [momentum[d]]
    for c in range(3):
        term = momentum[d] * velocity[c]
        carried.append(term + total_pressure if c == d else term)
    carried.append((energy + total_pressure) * speed)
    carried += [speed * field[c] for c in others]
    return conserved, carried, signal, projection


def twice_flux(lower, upper, normal, d):
    others = [c for c in range(3) if c != d]

    def field_of(state):
        field = [normal, normal, normal]
        for at, c in enumerate(others):
            field[c] = state[5 + at]
        return field

    field_low, field_up = field_of(lower), field_of(upper)
    u_low, f_low, s_low, j_low = state_terms(lower, field_low, d)
    u_up, f_up, s_up, j_up = state_terms(upper, field_up, d)
    signal = jnp.maximum(s_low, s_up)
    tension = [None]
    for c in range(3):
        tension.append(field_low[c] + field_up[c])
    tension.append(j_low + j_up)
    tension += [lower[1 + c] + upper[1 + c] for c in others]
    result = []
    for n in range(7):
        central = f_low[n] + f_up[n]
        if tension[n] is not None:
            central = central - normal * tension[n]
        result.append(central - signal * (u_up[n] - u_low[n]))
    return result


def at(ref, n, r, offset=0):
    return ref[n, pl.ds(r[0] + offset, r[1]), :]


def put(ref, n, r, value):
    ref[n, pl.ds(r[0], r[1]), :] = value


def blocks(begin, rows, count, body):
    def step(i, carry):
        body((pl.multiple_of(PAD + begin + i * rows, 8), rows))
        return carry

    if count == 1:
        step(0, 0)
    else:
        lax.fori_loop(0, count, step, 0)


def each_block(first, last, rows, body):
    begin = first * W // 8 * 8
    blocks(begin, rows, -(-(last * W - begin) // rows), body)


def cell_fields(q, r):
    put(q, 8, r, 0.5 * (at(q, 5, r) + at(q, 5, r, W)))
    put(q, 9, r, 0.5 * (at(q, 6, r) + at(q, 6, r, 1)))
    bz = at(q, 7, r)
    put(q, 10, r, 0.5 * (bz + up(bz)))


def changing(d):
    return list(range(5)) + [8 + c for c in range(3) if c != d]


def side_states(q, hi, d, offset, r, n, name):
    value = at(q, name, r)
    half = half_slope(value - at(q, name, r, -offset), at(q, name, r, offset) - value)
    put(hi, n, r, value + half)
    return value - half


def side_fluxes(q, hi, d, offset, target, r):
    upper = [side_states(q, hi, d, offset, r, n, name) for n, name in enumerate(changing(d))]
    lower = [at(hi, n, r, -offset) for n in range(7)]
    for n, value in enumerate(twice_flux(lower, upper, at(q, 5 + d, r), d)):
        put(target, n, r, value)


def stored_states(q, hi, d, offset, r):
    for n, name in enumerate(changing(d)):
        put(hi, 7 + n, r, side_states(q, hi, d, offset, r, n, name))


def stored_fluxes(q, hi, d, offset, target, r):
    upper = [at(hi, 7 + n, r) for n in range(7)]
    lower = [at(hi, n, r, -offset) for n in range(7)]
    for n, value in enumerate(twice_flux(lower, upper, at(q, 5 + d, r), d)):
        put(target, n, r, value)


def height_states(q, hi, r):
    for n, name in enumerate(changing(2)):
        value = at(q, name, r)
        before, earlier, after = down(value), down(value, 2), up(value)
        below = value - before
        put(hi, 7 + n, r, value - half_slope(below, after - value))
        put(hi, n, r, before + half_slope(before - earlier, below))


QUARTER = 0.125 * TIME_STEP


def edges(gx, gy, gz, edge, r):
    fx_z = at(gx, 6, r)
    fy_z = at(gy, 6, r)
    put(
        edge, 0, r, QUARTER * (at(gz, 6, r, -1) + at(gz, 6, r) - down(fy_z) - fy_z)
    )
    put(
        edge, 1, r, QUARTER * (down(fx_z) + fx_z - at(gz, 5, r, -W) - at(gz, 5, r))
    )
    put(
        edge,
        2,
        r,
        QUARTER * (at(gy, 5, r, -W) + at(gy, 5, r) - at(gx, 5, r, -1) - at(gx, 5, r)),
    )


def new_faces(q, edge, face, r):
    ex, ey, ez = at(edge, 0, r), at(edge, 1, r), at(edge, 2, r)
    put(face, 0, r, at(q, 5, r) - (at(edge, 2, r, 1) - ez) + (up(ey) - ey))
    put(face, 1, r, at(q, 6, r) - (up(ex) - ex) + (at(edge, 2, r, W) - ez))
    put(face, 2, r, at(q, 7, r) - (at(edge, 1, r, W) - ey) + (at(edge, 0, r, 1) - ex))


def put_temperature(heat, r, temperature):
    above, below = up(temperature), down(temperature)
    put(heat, 4, r, temperature)
    put(heat, 5, r, temperature + below)
    put(heat, 6, r, temperature - below)
    put(heat, 7, r, above - below)


def new_cells(q, gx, gy, gz, face, cell, heat, r):
    density = at(q, 0, r)
    momentum = [density * at(q, 1 + c, r) for c in range(3)]
    twice_kinetic = (
        momentum[0] * at(q, 1, r) + momentum[1] * at(q, 2, r) + momentum[2] * at(q, 3, r)
    )
    field_sq = (
        at(q, 8, r) * at(q, 8, r) + at(q, 9, r) * at(q, 9, r) + at(q, 10, r) * at(q, 10, r)
    )
    energy = 1.5 * at(q, 4, r) + 0.5 * (twice_kinetic + field_sq)
    updated = []
    for n, value in enumerate([density] + momentum + [energy]):
        change = (at(gx, n, r, W) - at(gx, n, r)) + (at(gy, n, r, 1) - at(gy, n, r))
        above = at(gz, n, r)
        updated.append(value - (0.5 * TIME_STEP) * (change + (up(above) - above)))
    floored = jnp.maximum(updated[0], DENSITY_FLOOR)
    inverse = 1.0 / floored
    velocity = [updated[1 + c] * inverse for c in range(3)]
    bz = at(face, 2, r)
    field = [
        0.5 * (at(face, 0, r) + at(face, 0, r, W)),
        0.5 * (at(face, 1, r) + at(face, 1, r, 1)),
        0.5 * (bz + up(bz)),
    ]
    twice_kinetic = (
        updated[1] * velocity[0] + updated[2] * velocity[1] + updated[3] * velocity[2]
    )
    field_sq = field[0] * field[0] + field[1] * field[1] + field[2] * field[2]
    internal = updated[4] - 0.5 * (twice_kinetic + field_sq)
    pressure = jnp.maximum((GAMMA_RATIO - 1.0) * internal, PRESSURE_FLOOR)
    temperature = pressure * inverse
    put(cell, 0, r, floored)
    for c in range(3):
        put(cell, 1 + c, r, velocity[c])
        put(cell, 6 + c, r, field[c])
    put(cell, 4, r, inverse)
    put(cell, 5, r, temperature * temperature * jnp.sqrt(temperature))
    put(heat, 0, r, pressure)
    put_temperature(heat, r, temperature)


def couple(face, cell, coupling, r):
    own_field = [at(cell, 6 + c, r) for c in range(3)]
    own_conduct = at(cell, 5, r)
    for d in range(3):
        if d < 2:
            offset = -W if d == 0 else -1
            beside = [at(cell, 6 + c, r, offset) for c in range(3)]
            conduct = at(cell, 5, r, offset)
        else:
            beside = [down(a) for a in own_field]
            conduct = down(own_conduct)
        normal = at(face, d, r)
        parts = [normal if c == d else 0.5 * (own_field[c] + beside[c]) for c in range(3)]
        size = parts[0] * parts[0] + parts[1] * parts[1] + parts[2] * parts[2]
        factor = 0.5 * (own_conduct + conduct) / jnp.maximum(size, FIELD_FLOOR) * normal
        mixed = 0.25 * factor
        for c in range(3):
            put(coupling, 3 * d + c, r, (factor if c == d else mixed) * parts[c])


def early_kernel(mid_ref, near_ref, q, gx, gy, gz, edge, face, cell, coupling, heat, hi, landed, arrived):
    even = is_even("gx")
    target = pl.multiple_of(PAD + jnp.where(even, SENT + MID, 0), 8)
    copy = pltpu.make_async_copy(near_ref, landed, arrived)
    copy.start()
    for n in range(8):
        q[n, PAD + SENT : PAD + SENT + MID] = mid_ref[n]

    def upright(begin):
        blocks(begin, MID, 1, lambda r: cell_fields(q, r))
        blocks(begin, 144, 1, lambda r: height_states(q, hi, r))
        blocks(begin, 48, 3, lambda r: stored_fluxes(q, hi, 2, 0, gz, r))
        blocks(begin, 48, 3, lambda r: side_fluxes(q, hi, 1, 1, gy, r))

    upright(SENT)
    copy.wait()
    for n in range(8):
        q[n, pl.ds(target, SENT), :] = landed[n]
    upright(jnp.where(even, 256, 0))
    base = jnp.where(even, SENT, 0)
    blocks(base + 16, 16, 16, lambda r: side_fluxes(q, hi, 0, W, gx, r))
    blocks(base + 40, 224, 1, lambda r: edges(gx, gy, gz, edge, r))
    blocks(base + 40, 224, 1, lambda r: new_faces(q, edge, face, r))
    blocks(base + 40, 200, 1, lambda r: new_cells(q, gx, gy, gz, face, cell, heat, r))
    blocks(base + 56, 184, 1, lambda r: couple(face, cell, coupling, r))


def main_kernel(far_ref, *refs):
    density_out, velocity_out, pressure_out, magnetic_out = refs[9:13]
    q, gx, gy, gz, edge, face, cell, coupling, heat, hi = refs[13:]
    even = is_even("gx")
    target = pl.multiple_of(PAD + jnp.where(even, 0, SENT + MID), 8)
    for n in range(8):
        q[n, pl.ds(target, SENT), :] = far_ref[n]

    def begin(of_even, of_odd):
        return jnp.where(even, of_even, of_odd)

    blocks(begin(0, 256), 144, 1, lambda r: cell_fields(q, r))
    blocks(begin(0, 256), 128, 1, lambda r: height_states(q, hi, r))
    blocks(begin(0, 256), FZ, 128 // FZ, lambda r: stored_fluxes(q, hi, 2, 0, gz, r))
    blocks(begin(0, 240), FY, 144 // FY, lambda r: side_fluxes(q, hi, 1, 1, gy, r))
    blocks(begin(16, 232), 152, 1, lambda r: stored_states(q, hi, 0, W, r))
    blocks(begin(40, 256), FX, 128 // FX, lambda r: stored_fluxes(q, hi, 0, W, gx, r))
    blocks(begin(40, 256), 128, 1, lambda r: edges(gx, gy, gz, edge, r))
    blocks(begin(40, 240), 144, 1, lambda r: new_faces(q, edge, face, r))
    blocks(begin(40, 240), 120, 1, lambda r: new_cells(q, gx, gy, gz, face, cell, heat, r))
    blocks(begin(56, 240), 128, 1, lambda r: couple(face, cell, coupling, r))

    def heat_fluxes(r):
        t = at(heat, 4, r)
        t_below_x = at(heat, 4, r, -W)
        t_below_y = at(heat, 4, r, -1)
        along_x = at(heat, 4, r, W) - t_below_x
        along_y = at(heat, 4, r, 1) - t_below_y
        along_z = at(heat, 7, r)
        beside_x = at(heat, 4, r, W - 1) - at(heat, 4, r, -W - 1)
        beside_y = at(heat, 4, r, 1 - W) - at(heat, 4, r, -1 - W)
        k = [at(coupling, n, r) for n in range(9)]
        qx = (
            k[0] * (t - t_below_x)
            + k[1] * (along_y + beside_y)
            + k[2] * (along_z + at(heat, 7, r, -W))
        )
        qy = (
            k[3] * (along_x + beside_x)
            + k[4] * (t - t_below_y)
            + k[5] * (along_z + at(heat, 7, r, -1))
        )
        qz = (
            k[6] * (at(heat, 5, r, W) - at(heat, 5, r, -W))
            + k[7] * (at(heat, 5, r, 1) - at(heat, 5, r, -1))
            + k[8] * at(heat, 6, r)
        )
        put(heat, 8, r, qx)
        put(heat, 9, r, qy)
        put(heat, 10, r, qz)

    def rate_at(r):
        qz = at(heat, 10, r)
        return (
            (at(heat, 8, r, W) - at(heat, 8, r)) + (at(heat, 9, r, 1) - at(heat, 9, r)) + (up(qz) - qz)
        )

    b = [1.0 / 3.0] * 3 + [(j * j + j - 2.0) / (2.0 * j * (j + 1.0)) for j in range(3, SECTIONS + 1)]
    base_rate = 4.0 / (SUPER_SECTIONS * SUPER_SECTIONS + SUPER_SECTIONS - 2.0)
    scale = (GAMMA_RATIO - 1.0) * SUPER_TIME * base_rate

    def section(j, r):
        rate = rate_at(r)
        if j == 1:
            put(heat, 11, r, rate)
            return at(heat, 0, r) + (b[1] * scale) * rate
        mu = (2.0 * j - 1.0) / j * b[j] / b[j - 1]
        nu = -(j - 1.0) / j * b[j] / b[j - 2]
        if j == 2:
            base = (1.0 - mu) * at(heat, 0, r)
        else:
            base = nu * at(heat, j - 2, r) + (1.0 - mu - nu) * at(heat, 0, r)
        return (
            mu * at(heat, j - 1, r)
            + base
            + (mu * scale) * rate
            - ((1.0 - b[j - 1]) * mu * scale) * at(heat, 11, r)
        )

    for j in range(1, SECTIONS):
        each_block(2 + j, W - 1 - j, FLOWS, heat_fluxes)

        def advance(r, j=j):
            pressure = section(j, r)
            put(heat, j, r, pressure)
            put_temperature(heat, r, pressure * at(cell, 4, r))

        each_block(2 + j, W - 2 - j, ADVANCE, advance)

    each_block(2 + SECTIONS, W - 1 - SECTIONS, FLOWS, heat_fluxes)

    for x in range(OWN):
        r = (PAD + (x + RIM) * W + RIM, OWN)
        pressure_out[x] = section(SECTIONS, r)
        density_out[x] = at(cell, 0, r)
        for c in range(3):
            velocity_out[c, x] = at(cell, 1 + c, r)
            magnetic_out[c, x] = at(face, c, r)


def kept(a):
    return pltpu.with_memory_space_constraint(a, pltpu.VMEM)


def in_vmem(*shape):
    return pltpu.VMEM(shape, jnp.float32)


def on_chip(kernel, name, arguments, shapes, scratch=(), limit=None, cost=None, anywhere=0):
    spec = pl.BlockSpec(memory_space=pltpu.VMEM)
    results = pl.pallas_call(
        kernel,
        in_specs=[spec] * (len(arguments) - anywhere)
        + [pl.BlockSpec(memory_space=pl.ANY)] * anywhere,
        out_specs=[spec] * len(shapes),
        out_shape=[in_vmem(*shape) for shape in shapes],
        scratch_shapes=[pltpu.VMEM(shape, jnp.float32) for shape in scratch]
        + [pltpu.SemaphoreType.DMA] * anywhere,
        compiler_params=pltpu.CompilerParams(vmem_limit_bytes=limit),
        cost_estimate=cost,
        name=name,
    )(*arguments)
    return [kept(a) for a in results]


def swapped(a, axis, near):
    count = lax.axis_size(axis)
    step = 1 if near else count - 1
    pairs = [(i, (i + (step if i % 2 == 0 else count - step)) % count) for i in range(count)]
    return kept(lax.ppermute(a, axis, pairs))


def main_call(far, buffers):
    spec = pl.BlockSpec(memory_space=pltpu.VMEM)
    block = (OWN, OWN, NZ)
    shapes = (block, (3, *block), block, (3, *block))
    return pl.pallas_call(
        main_kernel,
        in_specs=[spec] * (1 + len(buffers)),
        out_specs=[spec] * (4 + len(buffers)),
        out_shape=[jax.ShapeDtypeStruct(shape, jnp.float32) for shape in shapes]
        + [in_vmem(*a.shape) for a in buffers],
        input_output_aliases={1 + n: 4 + n for n in range(len(buffers))},
        scratch_shapes=[pltpu.VMEM((14, ROWS, NZ), jnp.float32)],
        compiler_params=pltpu.CompilerParams(vmem_limit_bytes=16 << 20),
        name="main",
    )(far, *buffers)[:4]


def local(*arguments):
    packed = (8, OWN * RIM, NZ)
    own, near, far = on_chip(pack_kernel, "pack", arguments, [(8, OWN * OWN, NZ), packed, packed])
    count = lax.axis_size("gy")
    far = kept(lax.ppermute(far, "gy", [(i, (i - 1) % count) for i in range(count)]))
    near = kept(lax.ppermute(near, "gy", [(i, (i + 1) % count) for i in range(count)]))
    message = (8, SENT, NZ)
    mid, sent, beside = on_chip(
        widen_kernel, "widen", (own, near, far), [(8, MID, NZ), message, message]
    )
    far = swapped(sent, "gx", False)
    near = lax.cond(
        lax.axis_index("gx") >= 0, lambda a: swapped(a, "gx", True), lambda a: a, beside
    )
    shapes = [(n, ROWS, NZ) for n in (11, 7, 7, 7, 3, 3, 9, 9, 12)]
    buffers = on_chip(early_kernel, "early", (mid, near), shapes, [(14, ROWS, NZ), message], 16 << 20, pl.CostEstimate(flops=0, bytes_accessed=1024, transcendentals=0), 1)
    return tuple(main_call(far, buffers))


def solution(mesh):
    grid = P("gx", "gy", None)
    stacked = P(None, "gx", "gy", None)
    return jax.shard_map(
        local,
        mesh=mesh,
        in_specs=(grid, stacked, grid, stacked),
        out_specs=(grid, stacked, grid, stacked),
        check_vma=False,
    )
```

```python
import jax
import jax.numpy as jnp
from jax import lax
from jax.experimental import pallas as pl
from jax.experimental.pallas import tpu as pltpu
from jax.sharding import PartitionSpec as P

SECTIONS = 4
SUPER_SECTIONS = 8
GAMMA_RATIO = 5.0 / 3.0
TIME_STEP = 0.04
SUPER_TIME = 0.08
DENSITY_FLOOR = 0.5
PRESSURE_FLOOR = 0.1
FIELD_FLOOR = 0.05

OWN = 8
RIM = 2 + SECTIONS
W = OWN + 2 * RIM
NZ = 128
PAD = 32
ROWS = PAD + W * W + 96
SENT = RIM * W
MID = OWN * W
FZ, FY, FX, FLOWS, ADVANCE = 32, 48, 32, 304, 288


def is_even(axis):
    return lax.axis_index(axis) % 2 == 0


def pack_kernel(mass_ref, velocity_ref, stress_ref, magnetic_ref, own_ref, near_ref, far_ref):
    for x in range(OWN):
        fields = [mass_ref[x]] + [velocity_ref[c, x] for c in range(3)]
        fields += [stress_ref[x]] + [magnetic_ref[c, x] for c in range(3)]
        for n, value in enumerate(fields):
            low, high = value[:RIM], value[OWN - RIM :]
            own_ref[n, OWN * x : OWN * (x + 1)] = value
            near_ref[n, RIM * x : RIM * (x + 1)] = high
            far_ref[n, RIM * x : RIM * (x + 1)] = low


def widen_kernel(own_ref, near_ref, far_ref, mid_ref, sent_ref, beside_ref):
    for x in range(OWN):
        for n in range(8):
            near = near_ref[n, RIM * x : RIM * (x + 1)]
            far = far_ref[n, RIM * x : RIM * (x + 1)]
            at = x * W
            mid_ref[n, at : at + RIM] = near
            mid_ref[n, at + RIM : at + RIM + OWN] = own_ref[n, OWN * x : OWN * (x + 1)]
            mid_ref[n, at + RIM + OWN : at + W] = far
    low = pl.multiple_of(jnp.where(is_even("gx"), 0, MID - SENT), 8)
    high = pl.multiple_of(jnp.where(is_even("gx"), MID - SENT, 0), 8)
    for n in range(8):
        sent_ref[n] = mid_ref[n, pl.ds(low, SENT), :]
        beside_ref[n] = mid_ref[n, pl.ds(high, SENT), :]


def up(a):
    return pltpu.roll(a, NZ - 1, 1)


def down(a, by=1):
    return pltpu.roll(a, by, 1)


def half_slope(below, above):
    slope = jnp.minimum(jnp.maximum(below, jnp.minimum(above, 0.0)), jnp.maximum(above, 0.0))
    return 0.5 * slope


def state_terms(state, field, d):
    density, velocity, pressure = state[0], state[1:4], state[4]
    magnetic_sq = field[0] * field[0] + field[1] * field[1] + field[2] * field[2]
    projection = velocity[0] * field[0] + velocity[1] * field[1] + velocity[2] * field[2]
    momentum = [density * velocity[c] for c in range(3)]
    twice_kinetic = (
        momentum[0] * velocity[0] + momentum[1] * velocity[1] + momentum[2] * velocity[2]
    )
    half_sq = 0.5 * magnetic_sq
    total_pressure = pressure + half_sq
    energy = 1.5 * pressure + (0.5 * twice_kinetic + half_sq)
    speed = velocity[d]
    wave_arg = GAMMA_RATIO * pressure + magnetic_sq
    signal = jnp.abs(speed) + wave_arg * lax.rsqrt(wave_arg * density)
    others = [c for c in range(3) if c != d]
    conserved = [density] + momentum + [energy] + [field[c] for c in others]
    carried = [momentum[d]]
    for c in range(3):
        term = momentum[d] * velocity[c]
        carried.append(term + total_pressure if c == d else term)
    carried.append((energy + total_pressure) * speed)
    carried += [speed * field[c] for c in others]
    return conserved, carried, signal, projection


def twice_flux(lower, upper, normal, d):
    others = [c for c in range(3) if c != d]

    def field_of(state):
        field = [normal, normal, normal]
        for at, c in enumerate(others):
            field[c] = state[5 + at]
        return field

    field_low, field_up = field_of(lower), field_of(upper)
    u_low, f_low, s_low, j_low = state_terms(lower, field_low, d)
    u_up, f_up, s_up, j_up = state_terms(upper, field_up, d)
    signal = jnp.maximum(s_low, s_up)
    tension = [None]
    for c in range(3):
        tension.append(field_low[c] + field_up[c])
    tension.append(j_low + j_up)
    tension += [lower[1 + c] + upper[1 + c] for c in others]
    result = []
    for n in range(7):
        central = f_low[n] + f_up[n]
        if tension[n] is not None:
            central = central - normal * tension[n]
        result.append(central - signal * (u_up[n] - u_low[n]))
    return result


def at(ref, n, r, offset=0):
    return ref[n, pl.ds(r[0] + offset, r[1]), :]


def put(ref, n, r, value):
    ref[n, pl.ds(r[0], r[1]), :] = value


def blocks(begin, rows, count, body):
    def step(i, carry):
        body((pl.multiple_of(PAD + begin + i * rows, 8), rows))
        return carry

    if count == 1:
        step(0, 0)
    else:
        lax.fori_loop(0, count, step, 0)


def each_block(first, last, rows, body):
    begin = first * W // 8 * 8
    blocks(begin, rows, -(-(last * W - begin) // rows), body)


def cell_fields(q, r):
    put(q, 8, r, 0.5 * (at(q, 5, r) + at(q, 5, r, W)))
    put(q, 9, r, 0.5 * (at(q, 6, r) + at(q, 6, r, 1)))
    bz = at(q, 7, r)
    put(q, 10, r, 0.5 * (bz + up(bz)))


def changing(d):
    return list(range(5)) + [8 + c for c in range(3) if c != d]


def side_states(q, hi, d, offset, r, n, name):
    value = at(q, name, r)
    half = half_slope(value - at(q, name, r, -offset), at(q, name, r, offset) - value)
    put(hi, n, r, value + half)
    return value - half


def side_fluxes(q, hi, d, offset, target, r):
    upper = [side_states(q, hi, d, offset, r, n, name) for n, name in enumerate(changing(d))]
    lower = [at(hi, n, r, -offset) for n in range(7)]
    for n, value in enumerate(twice_flux(lower, upper, at(q, 5 + d, r), d)):
        put(target, n, r, value)


def stored_states(q, hi, d, offset, r):
    for n, name in enumerate(changing(d)):
        put(hi, 7 + n, r, side_states(q, hi, d, offset, r, n, name))


def stored_fluxes(q, hi, d, offset, target, r):
    upper = [at(hi, 7 + n, r) for n in range(7)]
    lower = [at(hi, n, r, -offset) for n in range(7)]
    for n, value in enumerate(twice_flux(lower, upper, at(q, 5 + d, r), d)):
        put(target, n, r, value)


def height_states(q, hi, r):
    for n, name in enumerate(changing(2)):
        value = at(q, name, r)
        before, earlier, after = down(value), down(value, 2), up(value)
        below = value - before
        put(hi, 7 + n, r, value - half_slope(below, after - value))
        put(hi, n, r, before + half_slope(before - earlier, below))


QUARTER = 0.125 * TIME_STEP


def edges(gx, gy, gz, edge, r):
    fx_z = at(gx, 6, r)
    fy_z = at(gy, 6, r)
    put(
        edge, 0, r, QUARTER * (at(gz, 6, r, -1) + at(gz, 6, r) - down(fy_z) - fy_z)
    )
    put(
        edge, 1, r, QUARTER * (down(fx_z) + fx_z - at(gz, 5, r, -W) - at(gz, 5, r))
    )
    put(
        edge,
        2,
        r,
        QUARTER * (at(gy, 5, r, -W) + at(gy, 5, r) - at(gx, 5, r, -1) - at(gx, 5, r)),
    )


def new_faces(q, edge, face, r):
    ex, ey, ez = at(edge, 0, r), at(edge, 1, r), at(edge, 2, r)
    put(face, 0, r, at(q, 5, r) - (at(edge, 2, r, 1) - ez) + (up(ey) - ey))
    put(face, 1, r, at(q, 6, r) - (up(ex) - ex) + (at(edge, 2, r, W) - ez))
    put(face, 2, r, at(q, 7, r) - (at(edge, 1, r, W) - ey) + (at(edge, 0, r, 1) - ex))


def put_temperature(heat, r, temperature):
    above, below = up(temperature), down(temperature)
    put(heat, 4, r, temperature)
    put(heat, 5, r, temperature + below)
    put(heat, 6, r, temperature - below)
    put(heat, 7, r, above - below)


def new_cells(q, gx, gy, gz, face, cell, heat, r):
    density = at(q, 0, r)
    momentum = [density * at(q, 1 + c, r) for c in range(3)]
    twice_kinetic = (
        momentum[0] * at(q, 1, r) + momentum[1] * at(q, 2, r) + momentum[2] * at(q, 3, r)
    )
    field_sq = (
        at(q, 8, r) * at(q, 8, r) + at(q, 9, r) * at(q, 9, r) + at(q, 10, r) * at(q, 10, r)
    )
    energy = 1.5 * at(q, 4, r) + 0.5 * (twice_kinetic + field_sq)
    updated = []
    for n, value in enumerate([density] + momentum + [energy]):
        change = (at(gx, n, r, W) - at(gx, n, r)) + (at(gy, n, r, 1) - at(gy, n, r))
        above = at(gz, n, r)
        updated.append(value - (0.5 * TIME_STEP) * (change + (up(above) - above)))
    floored = jnp.maximum(updated[0], DENSITY_FLOOR)
    inverse = 1.0 / floored
    velocity = [updated[1 + c] * inverse for c in range(3)]
    bz = at(face, 2, r)
    field = [
        0.5 * (at(face, 0, r) + at(face, 0, r, W)),
        0.5 * (at(face, 1, r) + at(face, 1, r, 1)),
        0.5 * (bz + up(bz)),
    ]
    twice_kinetic = (
        updated[1] * velocity[0] + updated[2] * velocity[1] + updated[3] * velocity[2]
    )
    field_sq = field[0] * field[0] + field[1] * field[1] + field[2] * field[2]
    internal = updated[4] - 0.5 * (twice_kinetic + field_sq)
    pressure = jnp.maximum((GAMMA_RATIO - 1.0) * internal, PRESSURE_FLOOR)
    temperature = pressure * inverse
    put(cell, 0, r, floored)
    for c in range(3):
        put(cell, 1 + c, r, velocity[c])
        put(cell, 6 + c, r, field[c])
    put(cell, 4, r, inverse)
    put(cell, 5, r, temperature * temperature * jnp.sqrt(temperature))
    put(heat, 0, r, pressure)
    put_temperature(heat, r, temperature)


def couple(face, cell, coupling, r):
    own_field = [at(cell, 6 + c, r) for c in range(3)]
    own_conduct = at(cell, 5, r)
    for d in range(3):
        if d < 2:
            offset = -W if d == 0 else -1
            beside = [at(cell, 6 + c, r, offset) for c in range(3)]
            conduct = at(cell, 5, r, offset)
        else:
            beside = [down(a) for a in own_field]
            conduct = down(own_conduct)
        normal = at(face, d, r)
        parts = [normal if c == d else 0.5 * (own_field[c] + beside[c]) for c in range(3)]
        size = parts[0] * parts[0] + parts[1] * parts[1] + parts[2] * parts[2]
        factor = 0.5 * (own_conduct + conduct) / jnp.maximum(size, FIELD_FLOOR) * normal
        mixed = 0.25 * factor
        for c in range(3):
            put(coupling, 3 * d + c, r, (factor if c == d else mixed) * parts[c])


def early_kernel(mid_ref, near_ref, q, gx, gy, gz, edge, face, cell, coupling, heat, hi, landed, arrived):
    even = is_even("gx")
    target = pl.multiple_of(PAD + jnp.where(even, SENT + MID, 0), 8)
    copy = pltpu.make_async_copy(near_ref, landed, arrived)
    copy.start()
    for n in range(8):
        q[n, PAD + SENT : PAD + SENT + MID] = mid_ref[n]

    def upright(begin):
        blocks(begin, MID, 1, lambda r: cell_fields(q, r))
        blocks(begin, 144, 1, lambda r: height_states(q, hi, r))
        blocks(begin, 48, 3, lambda r: stored_fluxes(q, hi, 2, 0, gz, r))
        blocks(begin, 48, 3, lambda r: side_fluxes(q, hi, 1, 1, gy, r))

    upright(SENT)
    copy.wait()
    for n in range(8):
        q[n, pl.ds(target, SENT), :] = landed[n]
    upright(jnp.where(even, 256, 0))
    base = jnp.where(even, SENT, 0)
    blocks(base + 16, 32, 8, lambda r: side_fluxes(q, hi, 0, W, gx, r))
    blocks(base + 40, 224, 1, lambda r: edges(gx, gy, gz, edge, r))
    blocks(base + 40, 224, 1, lambda r: new_faces(q, edge, face, r))
    blocks(base + 40, 200, 1, lambda r: new_cells(q, gx, gy, gz, face, cell, heat, r))
    blocks(base + 56, 184, 1, lambda r: couple(face, cell, coupling, r))


def main_kernel(far_ref, *refs):
    density_out, velocity_out, pressure_out, magnetic_out = refs[9:13]
    q, gx, gy, gz, edge, face, cell, coupling, heat, hi = refs[13:]
    even = is_even("gx")
    target = pl.multiple_of(PAD + jnp.where(even, 0, SENT + MID), 8)
    for n in range(8):
        q[n, pl.ds(target, SENT), :] = far_ref[n]

    def begin(of_even, of_odd):
        return jnp.where(even, of_even, of_odd)

    blocks(begin(0, 256), 144, 1, lambda r: cell_fields(q, r))
    blocks(begin(0, 256), 128, 1, lambda r: height_states(q, hi, r))
    blocks(begin(0, 256), FZ, 128 // FZ, lambda r: stored_fluxes(q, hi, 2, 0, gz, r))
    blocks(begin(0, 240), FY, 144 // FY, lambda r: side_fluxes(q, hi, 1, 1, gy, r))
    blocks(begin(16, 232), 152, 1, lambda r: stored_states(q, hi, 0, W, r))
    blocks(begin(40, 256), FX, 128 // FX, lambda r: stored_fluxes(q, hi, 0, W, gx, r))
    blocks(begin(40, 256), 128, 1, lambda r: edges(gx, gy, gz, edge, r))
    blocks(begin(40, 240), 144, 1, lambda r: new_faces(q, edge, face, r))
    blocks(begin(40, 240), 120, 1, lambda r: new_cells(q, gx, gy, gz, face, cell, heat, r))
    blocks(begin(56, 240), 128, 1, lambda r: couple(face, cell, coupling, r))

    def heat_fluxes(r):
        t = at(heat, 4, r)
        t_below_x = at(heat, 4, r, -W)
        t_below_y = at(heat, 4, r, -1)
        along_x = at(heat, 4, r, W) - t_below_x
        along_y = at(heat, 4, r, 1) - t_below_y
        along_z = at(heat, 7, r)
        beside_x = at(heat, 4, r, W - 1) - at(heat, 4, r, -W - 1)
        beside_y = at(heat, 4, r, 1 - W) - at(heat, 4, r, -1 - W)
        k = [at(coupling, n, r) for n in range(9)]
        qx = (
            k[0] * (t - t_below_x)
            + k[1] * (along_y + beside_y)
            + k[2] * (along_z + at(heat, 7, r, -W))
        )
        qy = (
            k[3] * (along_x + beside_x)
            + k[4] * (t - t_below_y)
            + k[5] * (along_z + at(heat, 7, r, -1))
        )
        qz = (
            k[6] * (at(heat, 5, r, W) - at(heat, 5, r, -W))
            + k[7] * (at(heat, 5, r, 1) - at(heat, 5, r, -1))
            + k[8] * at(heat, 6, r)
        )
        put(heat, 8, r, qx)
        put(heat, 9, r, qy)
        put(heat, 10, r, qz)

    def rate_at(r):
        qz = at(heat, 10, r)
        return (
            (at(heat, 8, r, W) - at(heat, 8, r)) + (at(heat, 9, r, 1) - at(heat, 9, r)) + (up(qz) - qz)
        )

    b = [1.0 / 3.0] * 3 + [(j * j + j - 2.0) / (2.0 * j * (j + 1.0)) for j in range(3, SECTIONS + 1)]
    base_rate = 4.0 / (SUPER_SECTIONS * SUPER_SECTIONS + SUPER_SECTIONS - 2.0)
    scale = (GAMMA_RATIO - 1.0) * SUPER_TIME * base_rate

    def section(j, r):
        rate = rate_at(r)
        if j == 1:
            put(heat, 11, r, rate)
            return at(heat, 0, r) + (b[1] * scale) * rate
        mu = (2.0 * j - 1.0) / j * b[j] / b[j - 1]
        nu = -(j - 1.0) / j * b[j] / b[j - 2]
        if j == 2:
            base = (1.0 - mu) * at(heat, 0, r)
        else:
            base = nu * at(heat, j - 2, r) + (1.0 - mu - nu) * at(heat, 0, r)
        return (
            mu * at(heat, j - 1, r)
            + base
            + (mu * scale) * rate
            - ((1.0 - b[j - 1]) * mu * scale) * at(heat, 11, r)
        )

    for j in range(1, SECTIONS):
        each_block(2 + j, W - 1 - j, FLOWS, heat_fluxes)

        def advance(r, j=j):
            pressure = section(j, r)
            put(heat, j, r, pressure)
            put_temperature(heat, r, pressure * at(cell, 4, r))

        each_block(2 + j, W - 2 - j, ADVANCE, advance)

    each_block(2 + SECTIONS, W - 1 - SECTIONS, FLOWS, heat_fluxes)

    for x in range(OWN):
        r = (PAD + (x + RIM) * W + RIM, OWN)
        pressure_out[x] = section(SECTIONS, r)
        density_out[x] = at(cell, 0, r)
        for c in range(3):
            velocity_out[c, x] = at(cell, 1 + c, r)
            magnetic_out[c, x] = at(face, c, r)


def kept(a):
    return pltpu.with_memory_space_constraint(a, pltpu.VMEM)


def in_vmem(*shape):
    return pltpu.VMEM(shape, jnp.float32)


def on_chip(kernel, name, arguments, shapes, scratch=(), limit=None, cost=None, anywhere=0):
    spec = pl.BlockSpec(memory_space=pltpu.VMEM)
    results = pl.pallas_call(
        kernel,
        in_specs=[spec] * (len(arguments) - anywhere)
        + [pl.BlockSpec(memory_space=pl.ANY)] * anywhere,
        out_specs=[spec] * len(shapes),
        out_shape=[in_vmem(*shape) for shape in shapes],
        scratch_shapes=[pltpu.VMEM(shape, jnp.float32) for shape in scratch]
        + [pltpu.SemaphoreType.DMA] * anywhere,
        compiler_params=pltpu.CompilerParams(vmem_limit_bytes=limit),
        cost_estimate=cost,
        name=name,
    )(*arguments)
    return [kept(a) for a in results]


def swapped(a, axis, near):
    count = lax.axis_size(axis)
    step = 1 if near else count - 1
    pairs = [(i, (i + (step if i % 2 == 0 else count - step)) % count) for i in range(count)]
    return kept(lax.ppermute(a, axis, pairs))


def main_call(far, buffers):
    spec = pl.BlockSpec(memory_space=pltpu.VMEM)
    block = (OWN, OWN, NZ)
    shapes = (block, (3, *block), block, (3, *block))
    return pl.pallas_call(
        main_kernel,
        in_specs=[spec] * (1 + len(buffers)),
        out_specs=[spec] * (4 + len(buffers)),
        out_shape=[jax.ShapeDtypeStruct(shape, jnp.float32) for shape in shapes]
        + [in_vmem(*a.shape) for a in buffers],
        input_output_aliases={1 + n: 4 + n for n in range(len(buffers))},
        scratch_shapes=[pltpu.VMEM((14, ROWS, NZ), jnp.float32)],
        compiler_params=pltpu.CompilerParams(vmem_limit_bytes=16 << 20),
        name="main",
    )(far, *buffers)[:4]


def local(*arguments):
    packed = (8, OWN * RIM, NZ)
    own, near, far = on_chip(pack_kernel, "pack", arguments, [(8, OWN * OWN, NZ), packed, packed])
    count = lax.axis_size("gy")
    far = kept(lax.ppermute(far, "gy", [(i, (i - 1) % count) for i in range(count)]))
    near = kept(lax.ppermute(near, "gy", [(i, (i + 1) % count) for i in range(count)]))
    message = (8, SENT, NZ)
    mid, sent, beside = on_chip(
        widen_kernel, "widen", (own, near, far), [(8, MID, NZ), message, message]
    )
    far = swapped(sent, "gx", False)
    near = lax.cond(
        lax.axis_index("gx") >= 0, lambda a: swapped(a, "gx", True), lambda a: a, beside
    )
    shapes = [(n, ROWS, NZ) for n in (11, 7, 7, 7, 3, 3, 9, 9, 12)]
    buffers = on_chip(early_kernel, "early", (mid, near), shapes, [(14, ROWS, NZ), message], 16 << 20, pl.CostEstimate(flops=0, bytes_accessed=1024, transcendentals=0), 1)
    return tuple(main_call(far, buffers))


def solution(mesh):
    grid = P("gx", "gy", None)
    stacked = P(None, "gx", "gy", None)
    return jax.shard_map(
        local,
        mesh=mesh,
        in_specs=(grid, stacked, grid, stacked),
        out_specs=(grid, stacked, grid, stacked),
        check_vma=False,
    )
```
